256 devices in a mesh: pts: 64 (over y, z, core), grp: 4 (over x).
Axes of the slice: x: 4, y: 4, z: 8, core: 2. Of those that a mesh axis runs over, the one named last changes fastest.
Arguments:
- spectrum: float32 [4, 1152, 8192], P('grp', None, 'pts'), may hold values from 0.05 to 1
- coarse_spectra: float32 [4, 1152, 1024], P('grp', None, 'pts'), may hold values from 0.05 to 1
- wind_east: float32 [4, 8192], P('grp', 'pts'), may hold values from -6 to 6
- wind_north: float32 [4, 8192], P('grp', 'pts'), may hold values from -6 to 6
- refraction: float32 [4, 8192], P('grp', 'pts'), may hold values from -0.8 to 0.8
- freq_kernel: float32 [32, 32], replicated, may hold values from -1 to 1
- sea_mask: int32 [4, 8192], P('grp'), may hold values from 0 to 1, as said below
- upwind_lists: int32 [4, 4, 8192], P('grp'), may hold values from 0 to 9215, as said below
- boundary_list: int32 [4, 1024], P('grp', 'pts'), may hold values from 0 to 4095, as said below
Outputs:
- spectrum_out: float32 [4, 1152, 8192], P('grp', None, 'pts')
The draws below stay inside these ranges and needn't reach their ends.
Inputs may be any that keep to these rules, and one draw needn't show every extreme that they name: `sea_mask`: blocks of 128 points: the sea points of a block come first; some blocks are all land and some all sea. `upwind_lists`: A neighbour index below 8192 lies within 128 of the point's own index. A value 8192 + k names boundary point k, and k lies in k // 16 == (the point's index) // 128. `boundary_list`: boundary point k reads a coarse point j with (j % 1024) // 16 == k // 16.
All inputs are finite; a program needn't handle non-finite values.
Results may differ from the reference program's by a relative error of at most 0.0003.
Values sent between devices are 32-bit elements; how exact they have to be, the bound alone decides.
A program may use at most 64 MiB of HBM per device.

```python
import math
import jax
import jax.numpy as jnp
from jax import lax

NDIR = 36
NFREQ = 32
BLOCK = 128
NSUB = 2
NB_DEV = 16
CP_DEV = 16
COMP = 1152
PT_DEV = 128
GPTS = 8192
NB = 1024
CP = 1024
GROUPS = 4


def draw_sea_mask(key, part):
    first, second = jax.random.split(key)
    blocks = GPTS // BLOCK
    landing = jax.random.randint(first, (GROUPS, blocks), 0, 3)
    filled = jax.random.randint(second, (GROUPS, blocks), 1, BLOCK + 1)
    counts = jnp.where(landing == 0, 0, filled)
    counts = counts.at[0, 0].set(BLOCK)
    counts = counts.at[0, blocks - 1].set(0)
    inside = jnp.arange(BLOCK, dtype=jnp.int32)
    mask = (inside[None, None, :] < counts[:, :, None]).astype(jnp.int32)
    return mask.reshape(GROUPS, GPTS)


def draw_upwind_lists(key, part):
    first, second, third = jax.random.split(key, 3)
    points = jnp.arange(GPTS, dtype=jnp.int32)
    device = points // PT_DEV
    offsets = jax.random.randint(first, (GROUPS, 4, GPTS), -BLOCK, BLOCK + 1)
    nearby = jnp.clip(points[None, None, :] + offsets, 0, GPTS - 1)
    picking = jax.random.randint(second, (GROUPS, 4, GPTS), 0, 8)
    slots = jax.random.randint(third, (GROUPS, 4, GPTS), 0, NB_DEV)
    ghostly = GPTS + device[None, None, :] * NB_DEV + slots
    values = jnp.where(picking == 0, ghostly, nearby)
    inner = points % PT_DEV
    forced = GPTS + device * NB_DEV + inner
    values = values.at[:, 0, :].set(jnp.where(inner < NB_DEV, forced[None, :], values[:, 0, :]))
    values = values.at[:, 3, 0].set(0)
    return values.astype(jnp.int32)


def draw_boundary_list(key, part):
    first, second = jax.random.split(key)
    owners = jax.random.randint(first, (GROUPS, NB), 0, GROUPS)
    slots = jax.random.randint(second, (GROUPS, NB), 0, CP_DEV)
    device = jnp.arange(NB, dtype=jnp.int32) // NB_DEV
    values = owners * CP + device[None, :] * CP_DEV + slots
    values = values.at[0, 0].set(0)
    values = values.at[GROUPS - 1, NB - 1].set(GROUPS * CP - 1)
    return values.astype(jnp.int32)


def shard_levels(stream_key, shape, shards, smallest, top_value):
    gain, own = 1.0, jax.random.fold_in(stream_key, 6)
    for dim, shards_of in shards:
        draws = jnp.exp(jax.random.uniform(jax.random.fold_in(own, dim), (shards_of,), jnp.float32, smallest / len(shards), top_value / len(shards)))
        gain = gain * jnp.repeat(draws, shape[dim] // shards_of).reshape([-1 if axis == dim else 1 for axis in range(len(shape))])
    return gain


def centred(own_key, dims, deviation, bound, cuts=(), kind=jnp.bfloat16):
    factor_of = shard_levels(own_key, dims, cuts, -0.22, 0.18) if cuts else 1.0
    array = jax.random.normal(own_key, dims, jnp.float32) * deviation * factor_of
    return jnp.minimum(jnp.maximum(array, -bound), bound).astype(kind)


def setup_inputs(seed: int = 0) -> dict:
    seeds = jax.random.split(jax.random.key(seed), 10)
    spectrum = jnp.clip(jnp.exp(math.log(1.0) - 2.9957323 * jax.random.uniform(seeds[0], (GROUPS, COMP, GPTS), jnp.float32) ** shard_levels(seeds[0], (GROUPS, COMP, GPTS), ((0, 4), (2, 64)), -0.2, 0.2)), 0.05, 1.0)
    coarse_spectra = jnp.clip(jnp.exp(math.log(1.0) - 2.9957323 * jax.random.uniform(seeds[1], (GROUPS, COMP, CP), jnp.float32) ** shard_levels(seeds[1], (GROUPS, COMP, CP), ((0, 4), (2, 64)), -0.2, 0.2)), 0.05, 1.0)
    wind_east = centred(seeds[2], (GROUPS, GPTS), 1.5, 6.0, ((0, 4), (1, 64)), jnp.float32)
    wind_north = centred(seeds[3], (GROUPS, GPTS), 1.5, 6.0, ((0, 4), (1, 64)), jnp.float32)
    refraction = jnp.clip(jax.random.uniform(seeds[4], (GROUPS, GPTS), jnp.float32, -0.8, 0.8) * shard_levels(seeds[4], (GROUPS, GPTS), ((0, 4), (1, 64)), -0.4, 0.0), -0.8, 0.8)
    freq_kernel = centred(seeds[5], (NFREQ, NFREQ), NFREQ ** -0.5, 1.0, (), jnp.float32)
    sea_mask = draw_sea_mask(jax.random.fold_in(seeds[9], 71), 0)
    upwind_lists = draw_upwind_lists(jax.random.fold_in(seeds[9], 71), 0)
    boundary_list = draw_boundary_list(jax.random.fold_in(seeds[9], 71), 0)
    return {"spectrum": spectrum, "coarse_spectra": coarse_spectra, "wind_east": wind_east, "wind_north": wind_north, "refraction": refraction, "freq_kernel": freq_kernel, "sea_mask": sea_mask, "upwind_lists": upwind_lists, "boundary_list": boundary_list}


def tables(comp_ids):
    freq = (comp_ids // NDIR).astype(jnp.float32)
    dirn = (comp_ids % NDIR).astype(jnp.float32)
    theta = 2.0 * math.pi * (dirn + 0.5) / NDIR
    return freq, jnp.cos(theta), jnp.sin(theta)


def sources(spectra, east, north, maskf, kernel):
    freq, cosv, sinv = tables(jnp.arange(spectra.shape[0], dtype=jnp.int32))
    along = east[None, :] * cosv[:, None] + north[None, :] * sinv[:, None]
    grow = 0.1 * jax.nn.relu(along * jnp.power(1.1, 0.5 * freq)[:, None] - 1.0)
    etot = jnp.mean(spectra, axis=0)
    diss = 0.3 * etot[None, :] * (0.5 + freq / NFREQ)[:, None]
    mixed = jnp.dot(kernel, spectra.reshape(NFREQ, -1), precision=lax.Precision.HIGHEST).reshape(spectra.shape)
    return maskf[None, :] * (spectra + spectra * (grow - diss) + 0.2 * mixed)


def advect(extended, spectra, upwind, maskf, comp_ids):
    freq, cosv, sinv = tables(comp_ids)
    index_x = jnp.where(cosv[:, None] > 0, upwind[0][None, :], upwind[1][None, :])
    index_y = jnp.where(sinv[:, None] > 0, upwind[2][None, :], upwind[3][None, :])
    from_x = jnp.take_along_axis(extended, index_x, axis=1)
    from_y = jnp.take_along_axis(extended, index_y, axis=1)
    courant = 0.65 * jnp.power(1.1, -0.5 * freq)
    step_x = (courant * jnp.abs(cosv))[:, None]
    step_y = (courant * jnp.abs(sinv))[:, None]
    return maskf[None, :] * (spectra - step_x * (spectra - from_x) - step_y * (spectra - from_y))


def refract(spectra, turning, maskf):
    count = spectra.shape[1]
    freq = jnp.arange(NFREQ, dtype=jnp.int32).astype(jnp.float32)
    rate = turning[None, None, :] * (0.5 + 0.5 * jnp.power(1.1, -freq))[:, None, None]
    cube = spectra.reshape(NFREQ, NDIR, count)
    before = jnp.roll(cube, 1, axis=1)
    after = jnp.roll(cube, -1, axis=1)
    upwind = jnp.where(rate > 0, before, after)
    result = cube - jnp.abs(rate) * (cube - upwind)
    return maskf[None, :] * result.reshape(spectra.shape)


def reference(spectrum, coarse_spectra, wind_east, wind_north, refraction, freq_kernel, sea_mask, upwind_lists, boundary_list):
    flat_coarse = jnp.transpose(coarse_spectra, (1, 0, 2)).reshape(COMP, GROUPS * CP)
    comp_ids = jnp.arange(COMP, dtype=jnp.int32)
    results = []
    for group in range(GROUPS):
        maskf = sea_mask[group].astype(jnp.float32)
        ghost_rows = jnp.take(flat_coarse, boundary_list[group], axis=1)
        current = sources(spectrum[group], wind_east[group], wind_north[group], maskf, freq_kernel)
        for step in range(NSUB):
            extended = jnp.concatenate([current, ghost_rows], axis=1)
            current = advect(extended, current, upwind_lists[group], maskf, comp_ids)
        results.append(refract(current, refraction[group], maskf))
    return jnp.stack(results)
```

```python
import functools
import math

import jax
import jax.numpy as jnp
import numpy as np
from jax import lax
from jax.experimental import pallas as pl
from jax.experimental.pallas import tpu as pltpu
from jax.sharding import PartitionSpec as P

NDIR = 36
NFREQ = 32
BLOCK = 128
CHUNK = 3
NCHUNK = NDIR // CHUNK
MESH = pl.DeviceIdType.MESH


def kernel(
    n_pts,
    n_grp,
    trig_ref,
    spec_hbm,
    coarse_hbm,
    east_hbm,
    north_hbm,
    turn_hbm,
    kern_hbm,
    mask_hbm,
    lists_hbm,
    blist_hbm,
    out_ref,
    spec_v,
    winds_v,
    kern_v,
    mask_v,
    lists_v,
    blist_s,
    trig_s,
    coarse_v,
    coarse_n,
    lane_v,
    part_v,
    own,
    prv,
    nxt,
    load_sem,
    co_send,
    co_recv,
    send_sem,
    recv_sem,
):
    pos = lax.axis_index("pts")
    grp = lax.axis_index("grp")
    after = lax.rem(pos + 1, n_pts)
    before = lax.rem(pos + n_pts - 1, n_pts)
    group_points = mask_hbm.shape[1]
    ghosts = blist_hbm.shape[1]
    slots = coarse_hbm.shape[0]
    coarse_span = slots * n_pts

    here = pl.ds(pl.multiple_of(pos * BLOCK, BLOCK), BLOCK)
    loads = [
        pltpu.make_async_copy(spec_hbm, spec_v, load_sem.at[0]),
        pltpu.make_async_copy(coarse_hbm, coarse_v.at[grp], load_sem.at[1]),
        pltpu.make_async_copy(lists_hbm.at[:, here], lists_v, load_sem.at[2]),
        pltpu.make_async_copy(mask_hbm.at[:, here], mask_v, load_sem.at[3]),
        pltpu.make_async_copy(blist_hbm, blist_s, load_sem.at[4]),
        pltpu.make_async_copy(trig_ref, trig_s, load_sem.at[5]),
        pltpu.make_async_copy(east_hbm, winds_v.at[0], load_sem.at[6]),
        pltpu.make_async_copy(north_hbm, winds_v.at[1], load_sem.at[7]),
        pltpu.make_async_copy(turn_hbm, winds_v.at[2], load_sem.at[8]),
        pltpu.make_async_copy(kern_hbm, kern_v, load_sem.at[9]),
    ]
    for load in loads:
        load.start()

    barrier = pltpu.get_barrier_semaphore()
    pl.semaphore_signal(barrier, inc=1, device_id={"pts": after}, device_id_type=MESH)
    pl.semaphore_signal(barrier, inc=1, device_id={"pts": before}, device_id_type=MESH)
    for k in range(1, n_grp):
        peer = lax.rem(grp + k, n_grp)
        pl.semaphore_signal(barrier, inc=1, device_id={"grp": peer}, device_id_type=MESH)

    for load in loads[1:]:
        load.wait()
    lists = lists_v[...]
    shape = (4, BLOCK)
    slot = lists - (group_points + pos * ghosts)
    column = jnp.zeros(shape, jnp.int32)
    for k in range(ghosts):
        j = blist_s[0, k]
        col = lax.div(j, jnp.int32(coarse_span)) * slots + lax.rem(j, jnp.int32(slots))
        column = jnp.where(slot == k, col, column)
    rel = lists - (pos * BLOCK - BLOCK)
    is_far = lists >= group_points
    part = jnp.where(is_far, 3, lax.shift_right_arithmetic(rel, 7))
    lane = jnp.where(is_far, column, rel & 127)
    for r in range(4):
        lane_v[r] = jnp.broadcast_to(lane[r : r + 1], (NFREQ, BLOCK))
        part_v[r] = jnp.broadcast_to(part[r : r + 1], (NFREQ, BLOCK))

    maskf = jnp.broadcast_to(mask_v[...].astype(jnp.float32), (NFREQ, BLOCK))
    freq = lax.broadcasted_iota(jnp.int32, (NFREQ, BLOCK), 0).astype(jnp.float32)
    half_up = jnp.exp(freq * (0.5 * math.log(1.1)))
    courant = 0.65 * jnp.exp(freq * (-0.5 * math.log(1.1)))
    turn_factor = 0.5 + 0.5 * jnp.exp(freq * (-math.log(1.1)))

    loads[0].wait()
    comps = spec_v.shape[0]
    group_rows = 72

    def add_rows(i, acc):
        rows = spec_v[pl.ds(pl.multiple_of(i * group_rows, 8), group_rows), :]
        return acc + jnp.sum(rows.reshape(group_rows // 8, 8, BLOCK), axis=0)

    total = lax.fori_loop(0, comps // group_rows, add_rows, jnp.zeros((8, BLOCK), jnp.float32))
    etot = jnp.sum(total, axis=0, keepdims=True) * (1.0 / comps)
    diss = jnp.broadcast_to(0.3 * etot, (NFREQ, BLOCK)) * (0.5 + freq * (1.0 / NFREQ))

    pl.semaphore_wait(barrier, 2 + n_grp - 1)

    def coarse_copy(k):
        return pltpu.make_async_remote_copy(
            src_ref=coarse_hbm,
            dst_ref=coarse_v.at[grp],
            send_sem=co_send.at[k - 1],
            recv_sem=co_recv.at[k - 1],
            device_id={"grp": lax.rem(grp + k, n_grp)},
            device_id_type=MESH,
        )

    for k in range(1, n_grp):
        coarse_copy(k).start()

    def halo(step, c, way):
        rows = pl.ds(c * CHUNK, CHUNK)
        into = prv if way == 0 else nxt
        return pltpu.make_async_remote_copy(
            src_ref=own.at[step, rows],
            dst_ref=into.at[step, rows],
            send_sem=send_sem.at[step, way, c],
            recv_sem=recv_sem.at[step, way, c],
            device_id={"pts": after if way == 0 else before},
            device_id_type=MESH,
        )

    east = jnp.broadcast_to(winds_v[0], (NFREQ, BLOCK))
    north = jnp.broadcast_to(winds_v[1], (NFREQ, BLOCK))
    kern = kern_v[...]

    def source_chunk(c, carry):
        cells = [
            spec_v[pl.ds(c * CHUNK + i, NFREQ, stride=NDIR), :] for i in range(CHUNK)
        ]
        mixed = jnp.dot(
            kern,
            jnp.concatenate(cells, axis=1),
            precision=lax.Precision.HIGHEST,
            preferred_element_type=jnp.float32,
        )
        for i in range(CHUNK):
            d = c * CHUNK + i
            cell = cells[i]
            along = east * trig_s[0, d] + north * trig_s[1, d]
            grow = 0.1 * jnp.maximum(along * half_up - 1.0, 0.0)
            mix = mixed[:, i * BLOCK : (i + 1) * BLOCK]
            own[0, d] = maskf * (cell + cell * (grow - diss) + 0.2 * mix)
        halo(0, c, 0).start()
        halo(0, c, 1).start()
        return carry

    lax.fori_loop(0, NCHUNK, source_chunk, 0)

    for k in range(1, n_grp):
        coarse_copy(k).wait_recv()
    wide = coarse_v[...].reshape(n_grp * slots, comps)
    pad = jnp.zeros((BLOCK - n_grp * slots, BLOCK), jnp.float32)
    for t in range(comps // BLOCK):
        tile = jnp.concatenate([wide[:, t * BLOCK : (t + 1) * BLOCK], pad], axis=0)
        coarse_n[t * BLOCK : (t + 1) * BLOCK, :] = jnp.transpose(tile)

    def advect(step, c):
        quad = lax.div(c * CHUNK, 9)
        list_x = lax.rem(lax.div(quad + 1, 2), 2)
        list_y = 2 + lax.div(quad, 2)
        tables = []
        for which in (list_x, list_y):
            part_w = part_v[which]
            tables.append((lane_v[which], part_w == 0, part_w == 1, part_w == 2))
        results = []
        for i in range(CHUNK):
            d = c * CHUNK + i
            mine = own[step, d]
            sources = (
                prv[step, d],
                mine,
                nxt[step, d],
                coarse_n[pl.ds(d, NFREQ, stride=NDIR), :],
            )
            found = []
            for lane_w, p0, p1, p2 in tables:
                got = [
                    jnp.take_along_axis(source, lane_w, axis=1) for source in sources
                ]
                found.append(
                    jnp.where(p0, got[0], jnp.where(p1, got[1], jnp.where(p2, got[2], got[3])))
                )
            step_x = courant * trig_s[2, d]
            step_y = courant * trig_s[3, d]
            results.append(
                maskf * (mine - step_x * (mine - found[0]) - step_y * (mine - found[1]))
            )
        return results

    def first_chunk(c, carry):
        halo(0, c, 0).wait_recv()
        halo(0, c, 1).wait_recv()
        results = advect(0, c)
        for i in range(CHUNK):
            own[1, c * CHUNK + i] = results[i]
        halo(1, c, 0).start()
        halo(1, c, 1).start()
        return carry

    lax.fori_loop(0, NCHUNK, first_chunk, 0)

    rate = jnp.broadcast_to(winds_v[2], (NFREQ, BLOCK)) * turn_factor
    slow = jnp.abs(rate)
    turning_up = rate > 0

    def refract(d, low, high):
        mine = own[2, d]
        up = jnp.where(turning_up, own[2, low], own[2, high])
        out_ref[pl.ds(d, NFREQ, stride=NDIR), :] = maskf * (mine - slow * (mine - up))

    def second_chunk(c, carry):
        halo(1, c, 0).wait_recv()
        halo(1, c, 1).wait_recv()
        results = advect(1, c)
        for i in range(CHUNK):
            own[2, c * CHUNK + i] = results[i]
        return carry

    def second_and_turn(c, carry):
        second_chunk(c, carry)
        for i in range(CHUNK):
            d = c * CHUNK + i - 1
            refract(d, d - 1, d + 1)
        return carry

    second_chunk(0, 0)
    refract(1, 0, 2)
    lax.fori_loop(1, NCHUNK, second_and_turn, 0)
    refract(0, NDIR - 1, 1)
    refract(NDIR - 1, NDIR - 2, 0)

    def drain(c, carry):
        for step in range(2):
            for way in range(2):
                halo(step, c, way).wait_send()
        return carry

    lax.fori_loop(0, NCHUNK, drain, 0)
    for k in range(1, n_grp):
        coarse_copy(k).wait_send()


def trig_table():
    theta = 2.0 * math.pi * (np.arange(NDIR) + 0.5) / NDIR
    rows = [np.cos(theta), np.sin(theta), np.abs(np.cos(theta)), np.abs(np.sin(theta))]
    return np.stack(rows).astype(np.float32)


def shards(
    n_pts,
    n_grp,
    spectrum,
    coarse_spectra,
    wind_east,
    wind_north,
    refraction,
    freq_kernel,
    sea_mask,
    upwind_lists,
    boundary_list,
):
    comps = spectrum.shape[1]
    slots = coarse_spectra.shape[2]
    ghosts = boundary_list.shape[1]
    anyspace = pl.BlockSpec(memory_space=pl.ANY)
    block = (NDIR, NFREQ, BLOCK)
    out = pl.pallas_call(
        functools.partial(kernel, n_pts, n_grp),
        out_shape=jax.ShapeDtypeStruct((comps, BLOCK), jnp.float32),
        in_specs=[anyspace] * 10,
        out_specs=pl.BlockSpec(memory_space=pltpu.VMEM),
        scratch_shapes=[
            pltpu.VMEM((comps, BLOCK), jnp.float32),
            pltpu.VMEM((3, 1, BLOCK), jnp.float32),
            pltpu.VMEM((NFREQ, NFREQ), jnp.float32),
            pltpu.VMEM((1, BLOCK), jnp.int32),
            pltpu.VMEM((4, BLOCK), jnp.int32),
            pltpu.SMEM((1, ghosts), jnp.int32),
            pltpu.SMEM((4, NDIR), jnp.float32),
            pltpu.VMEM((n_grp, slots, comps), jnp.float32),
            pltpu.VMEM((comps, BLOCK), jnp.float32),
            pltpu.VMEM((4, NFREQ, BLOCK), jnp.int32),
            pltpu.VMEM((4, NFREQ, BLOCK), jnp.int32),
            pltpu.VMEM((3,) + block, jnp.float32),
            pltpu.VMEM((2,) + block, jnp.float32),
            pltpu.VMEM((2,) + block, jnp.float32),
            pltpu.SemaphoreType.DMA((10,)),
            pltpu.SemaphoreType.DMA((n_grp - 1,)),
            pltpu.SemaphoreType.DMA((n_grp - 1,)),
            pltpu.SemaphoreType.DMA((2, 2, NCHUNK)),
            pltpu.SemaphoreType.DMA((2, 2, NCHUNK)),
        ],
        compiler_params=pltpu.CompilerParams(
            collective_id=0, has_side_effects=True, vmem_limit_bytes=24 * 1024 * 1024
        ),
        name="wave_step",
    )(
        jnp.asarray(trig_table()),
        spectrum[0],
        jnp.transpose(coarse_spectra[0]),
        wind_east,
        wind_north,
        refraction,
        freq_kernel,
        sea_mask,
        upwind_lists[0],
        boundary_list,
    )
    return out[None]


def solution(mesh):
    placed = (
        P("grp", None, "pts"),
        P("grp", None, "pts"),
        P("grp", "pts"),
        P("grp", "pts"),
        P("grp", "pts"),
        P(),
        P("grp", None),
        P("grp", None, None),
        P("grp", "pts"),
    )
    return jax.shard_map(
        functools.partial(shards, mesh.shape["pts"], mesh.shape["grp"]),
        mesh=mesh,
        in_specs=placed,
        out_specs=P("grp", None, "pts"),
        check_vma=False,
    )
```

```python
import functools
import math

import jax
import jax.numpy as jnp
import numpy as np
from jax import lax
from jax.experimental import pallas as pl
from jax.experimental.pallas import tpu as pltpu
from jax.sharding import PartitionSpec as P

NDIR = 36
NFREQ = 32
BLOCK = 128
CHUNK = 3
NCHUNK = NDIR // CHUNK
MESH = pl.DeviceIdType.MESH


def kernel(
    n_pts,
    n_grp,
    trig_ref,
    spec_hbm,
    coarse_hbm,
    east_hbm,
    north_hbm,
    turn_hbm,
    kern_hbm,
    mask_hbm,
    lists_hbm,
    blist_hbm,
    out_ref,
    spec_v,
    winds_v,
    kern_v,
    mask_v,
    lists_v,
    blist_s,
    trig_s,
    coarse_v,
    coarse_n,
    pick_v,
    own,
    prv,
    nxt,
    load_sem,
    co_send,
    co_recv,
    send_sem,
    recv_sem,
):
    pos = lax.axis_index("pts")
    grp = lax.axis_index("grp")
    after = lax.rem(pos + 1, n_pts)
    before = lax.rem(pos + n_pts - 1, n_pts)
    group_points = mask_hbm.shape[1]
    ghosts = blist_hbm.shape[1]
    slots = coarse_hbm.shape[0]
    coarse_span = slots * n_pts

    here = pl.ds(pl.multiple_of(pos * BLOCK, BLOCK), BLOCK)
    loads = [
        pltpu.make_async_copy(spec_hbm, spec_v, load_sem.at[0]),
        pltpu.make_async_copy(coarse_hbm, coarse_v.at[grp], load_sem.at[1]),
        pltpu.make_async_copy(lists_hbm.at[:, here], lists_v, load_sem.at[2]),
        pltpu.make_async_copy(mask_hbm.at[:, here], mask_v, load_sem.at[3]),
        pltpu.make_async_copy(blist_hbm, blist_s, load_sem.at[4]),
        pltpu.make_async_copy(trig_ref, trig_s, load_sem.at[5]),
        pltpu.make_async_copy(east_hbm, winds_v.at[0], load_sem.at[6]),
        pltpu.make_async_copy(north_hbm, winds_v.at[1], load_sem.at[7]),
        pltpu.make_async_copy(turn_hbm, winds_v.at[2], load_sem.at[8]),
        pltpu.make_async_copy(kern_hbm, kern_v, load_sem.at[9]),
    ]
    for load in loads:
        load.start()

    barrier = pltpu.get_barrier_semaphore()
    pl.semaphore_signal(barrier, inc=1, device_id={"pts": after}, device_id_type=MESH)
    pl.semaphore_signal(barrier, inc=1, device_id={"pts": before}, device_id_type=MESH)
    for k in range(1, n_grp):
        peer = lax.rem(grp + k, n_grp)
        pl.semaphore_signal(barrier, inc=1, device_id={"grp": peer}, device_id_type=MESH)

    for load in loads[1:]:
        load.wait()
    lists = lists_v[...]
    shape = (4, BLOCK)
    slot = lists - (group_points + pos * ghosts)
    column = jnp.zeros(shape, jnp.int32)
    for k in range(ghosts):
        j = blist_s[0, k]
        col = lax.div(j, jnp.int32(coarse_span)) * slots + lax.rem(j, jnp.int32(slots))
        column = jnp.where(slot == k, col, column)
    rel = lists - (pos * BLOCK - BLOCK)
    is_far = lists >= group_points
    part = jnp.where(is_far, 3, lax.shift_right_arithmetic(rel, 7))
    lane = jnp.where(is_far, column, rel & 127)
    place = part * BLOCK + lane

    maskf = jnp.broadcast_to(mask_v[...].astype(jnp.float32), (NFREQ, BLOCK))
    freq = lax.broadcasted_iota(jnp.int32, (NFREQ, BLOCK), 0).astype(jnp.float32)
    half_up = jnp.exp(freq * (0.5 * math.log(1.1)))
    courant = 0.65 * jnp.exp(freq * (-0.5 * math.log(1.1)))
    turn_factor = 0.5 + 0.5 * jnp.exp(freq * (-math.log(1.1)))

    loads[0].wait()
    comps = spec_v.shape[0]
    group_rows = 72

    def add_rows(i, acc):
        rows = spec_v[pl.ds(pl.multiple_of(i * group_rows, 8), group_rows), :]
        return acc + jnp.sum(rows.reshape(group_rows // 8, 8, BLOCK), axis=0)

    total = lax.fori_loop(0, comps // group_rows, add_rows, jnp.zeros((8, BLOCK), jnp.float32))
    etot = jnp.sum(total, axis=0, keepdims=True) * (1.0 / comps)
    diss = jnp.broadcast_to(0.3 * etot, (NFREQ, BLOCK)) * (0.5 + freq * (1.0 / NFREQ))

    pl.semaphore_wait(barrier, 2 + n_grp - 1)

    def coarse_copy(k):
        return pltpu.make_async_remote_copy(
            src_ref=coarse_hbm,
            dst_ref=coarse_v.at[grp],
            send_sem=co_send.at[k - 1],
            recv_sem=co_recv.at[k - 1],
            device_id={"grp": lax.rem(grp + k, n_grp)},
            device_id_type=MESH,
        )

    for k in range(1, n_grp):
        coarse_copy(k).start()

    def halo(step, c, way):
        rows = pl.ds(c * CHUNK, CHUNK)
        into = prv if way == 0 else nxt
        return pltpu.make_async_remote_copy(
            src_ref=own.at[step, rows],
            dst_ref=into.at[step, rows],
            send_sem=send_sem.at[step, way, c],
            recv_sem=recv_sem.at[step, way, c],
            device_id={"pts": after if way == 0 else before},
            device_id_type=MESH,
        )

    east = jnp.broadcast_to(winds_v[0], (NFREQ, BLOCK))
    north = jnp.broadcast_to(winds_v[1], (NFREQ, BLOCK))
    kern_f = kern_v[...]
    kern_hi = kern_f.astype(jnp.bfloat16)
    kern_lo = (kern_f - kern_hi.astype(jnp.float32)).astype(jnp.bfloat16)
    kern = jnp.concatenate([kern_hi, kern_hi, kern_lo, kern_lo], axis=1)

    def send_both(step, c):
        @pl.when(pos < n_pts - 1)
        def _():
            halo(step, c, 0).start()

        @pl.when(pos > 0)
        def _():
            halo(step, c, 1).start()

    def await_both(step, c):
        @pl.when(pos > 0)
        def _():
            halo(step, c, 0).wait_recv()

        @pl.when(pos < n_pts - 1)
        def _():
            halo(step, c, 1).wait_recv()

    def sent_both(step, c):
        @pl.when(pos < n_pts - 1)
        def _():
            halo(step, c, 0).wait_send()

        @pl.when(pos > 0)
        def _():
            halo(step, c, 1).wait_send()

    def source_chunk(c, carry):
        cells = [
            spec_v[pl.ds(c * CHUNK + i, NFREQ, stride=NDIR), :] for i in range(CHUNK)
        ]
        wide = jnp.concatenate(cells, axis=1)
        wide_hi = wide.astype(jnp.bfloat16)
        wide_lo = (wide - wide_hi.astype(jnp.float32)).astype(jnp.bfloat16)
        mixed = jnp.dot(
            kern,
            jnp.concatenate([wide_hi, wide_lo, wide_hi, wide_lo], axis=0),
            preferred_element_type=jnp.float32,
        )
        for i in range(CHUNK):
            d = c * CHUNK + i
            cell = cells[i]
            along = east * trig_s[0, d] + north * trig_s[1, d]
            grow = 0.1 * jnp.maximum(along * half_up - 1.0, 0.0)
            mix = mixed[:, i * BLOCK : (i + 1) * BLOCK]
            own[0, d] = maskf * (cell + cell * (grow - diss) + 0.2 * mix)
        send_both(0, c)
        return carry

    lax.fori_loop(0, NCHUNK, source_chunk, 0)

    def clear(into):
        def clear_one(d, carry):
            for step in range(2):
                into[step, d] = jnp.zeros((NFREQ, BLOCK), jnp.float32)
            return carry

        lax.fori_loop(0, NDIR, clear_one, 0)

    @pl.when(pos == 0)
    def _():
        clear(prv)

    @pl.when(pos == n_pts - 1)
    def _():
        clear(nxt)

    window = lax.broadcasted_iota(jnp.int32, (4 * BLOCK, BLOCK), 0)
    for r in range(4):
        pick_v[r] = jnp.where(window == place[r : r + 1], 1.0, 0.0).astype(jnp.bfloat16)

    for k in range(1, n_grp):
        coarse_copy(k).wait_recv()
    wide = coarse_v[...].reshape(n_grp * slots, comps)
    pad = jnp.zeros((BLOCK - n_grp * slots, BLOCK), jnp.float32)
    for t in range(comps // BLOCK):
        tile = jnp.concatenate([wide[:, t * BLOCK : (t + 1) * BLOCK], pad], axis=0)
        coarse_n[t * BLOCK : (t + 1) * BLOCK, :] = jnp.transpose(tile)

    def advect(step, c):
        quad = lax.div(c * CHUNK, 9)
        list_x = lax.rem(lax.div(quad + 1, 2), 2)
        list_y = 2 + lax.div(quad, 2)
        picks = jnp.concatenate([pick_v[list_x], pick_v[list_y]], axis=1)
        mine = [own[step, c * CHUNK + i] for i in range(CHUNK)]
        rows = CHUNK * NFREQ
        here_rows = pl.ds(c * CHUNK, CHUNK)
        windows = jnp.concatenate(
            [
                prv[step, here_rows].reshape(rows, BLOCK),
                own[step, here_rows].reshape(rows, BLOCK),
                nxt[step, here_rows].reshape(rows, BLOCK),
                jnp.concatenate(
                    [
                        coarse_n[pl.ds(c * CHUNK + i, NFREQ, stride=NDIR), :]
                        for i in range(CHUNK)
                    ],
                    axis=0,
                ),
            ],
            axis=1,
        )
        high = windows.astype(jnp.bfloat16)
        low = (windows - high.astype(jnp.float32)).astype(jnp.bfloat16)
        found = jnp.dot(high, picks, preferred_element_type=jnp.float32) + jnp.dot(
            low, picks, preferred_element_type=jnp.float32
        )
        results = []
        for i in range(CHUNK):
            d = c * CHUNK + i
            cell = mine[i]
            from_x = found[i * NFREQ : (i + 1) * NFREQ, :BLOCK]
            from_y = found[i * NFREQ : (i + 1) * NFREQ, BLOCK:]
            step_x = courant * trig_s[2, d]
            step_y = courant * trig_s[3, d]
            results.append(
                maskf * (cell - step_x * (cell - from_x) - step_y * (cell - from_y))
            )
        return results

    def first_chunk(c, carry):
        await_both(0, c)
        results = advect(0, c)
        for i in range(CHUNK):
            own[1, c * CHUNK + i] = results[i]
        send_both(1, c)
        return carry

    lax.fori_loop(0, NCHUNK, first_chunk, 0)

    rate = jnp.broadcast_to(winds_v[2], (NFREQ, BLOCK)) * turn_factor
    slow = jnp.abs(rate)
    turning_up = rate > 0

    def refract(d, low, high):
        mine = own[2, d]
        up = jnp.where(turning_up, own[2, low], own[2, high])
        out_ref[pl.ds(d, NFREQ, stride=NDIR), :] = maskf * (mine - slow * (mine - up))

    def second_chunk(c, carry):
        await_both(1, c)
        results = advect(1, c)
        for i in range(CHUNK):
            own[2, c * CHUNK + i] = results[i]
        return carry

    def second_and_turn(c, carry):
        second_chunk(c, carry)
        for i in range(CHUNK):
            d = c * CHUNK + i - 1
            refract(d, d - 1, d + 1)
        return carry

    second_chunk(0, 0)
    refract(1, 0, 2)
    lax.fori_loop(1, NCHUNK, second_and_turn, 0)
    refract(0, NDIR - 1, 1)
    refract(NDIR - 1, NDIR - 2, 0)

    def drain(c, carry):
        for step in range(2):
            sent_both(step, c)
        return carry

    lax.fori_loop(0, NCHUNK, drain, 0)
    for k in range(1, n_grp):
        coarse_copy(k).wait_send()


def trig_table():
    theta = 2.0 * math.pi * (np.arange(NDIR) + 0.5) / NDIR
    rows = [np.cos(theta), np.sin(theta), np.abs(np.cos(theta)), np.abs(np.sin(theta))]
    return np.stack(rows).astype(np.float32)


def shards(
    n_pts,
    n_grp,
    spectrum,
    coarse_spectra,
    wind_east,
    wind_north,
    refraction,
    freq_kernel,
    sea_mask,
    upwind_lists,
    boundary_list,
):
    comps = spectrum.shape[1]
    slots = coarse_spectra.shape[2]
    ghosts = boundary_list.shape[1]
    anyspace = pl.BlockSpec(memory_space=pl.ANY)
    block = (NDIR, NFREQ, BLOCK)
    out = pl.pallas_call(
        functools.partial(kernel, n_pts, n_grp),
        out_shape=jax.ShapeDtypeStruct((comps, BLOCK), jnp.float32),
        in_specs=[anyspace] * 10,
        out_specs=pl.BlockSpec(memory_space=pltpu.VMEM),
        scratch_shapes=[
            pltpu.VMEM((comps, BLOCK), jnp.float32),
            pltpu.VMEM((3, 1, BLOCK), jnp.float32),
            pltpu.VMEM((NFREQ, NFREQ), jnp.float32),
            pltpu.VMEM((1, BLOCK), jnp.int32),
            pltpu.VMEM((4, BLOCK), jnp.int32),
            pltpu.SMEM((1, ghosts), jnp.int32),
            pltpu.SMEM((4, NDIR), jnp.float32),
            pltpu.VMEM((n_grp, slots, comps), jnp.float32),
            pltpu.VMEM((comps, BLOCK), jnp.float32),
            pltpu.VMEM((4, 4 * BLOCK, BLOCK), jnp.bfloat16),
            pltpu.VMEM((3,) + block, jnp.float32),
            pltpu.VMEM((2,) + block, jnp.float32),
            pltpu.VMEM((2,) + block, jnp.float32),
            pltpu.SemaphoreType.DMA((10,)),
            pltpu.SemaphoreType.DMA((n_grp - 1,)),
            pltpu.SemaphoreType.DMA((n_grp - 1,)),
            pltpu.SemaphoreType.DMA((2, 2, NCHUNK)),
            pltpu.SemaphoreType.DMA((2, 2, NCHUNK)),
        ],
        compiler_params=pltpu.CompilerParams(
            collective_id=0, has_side_effects=True, vmem_limit_bytes=24 * 1024 * 1024
        ),
        name="wave_step",
    )(*[pltpu.with_memory_space_constraint(a, pltpu.HBM) for a in (
        jnp.asarray(trig_table()),
        spectrum[0],
        jnp.transpose(coarse_spectra[0]),
        wind_east,
        wind_north,
        refraction,
        freq_kernel,
        sea_mask,
        upwind_lists[0],
        boundary_list,
    )])
    return out[None]


def solution(mesh):
    placed = (
        P("grp", None, "pts"),
        P("grp", None, "pts"),
        P("grp", "pts"),
        P("grp", "pts"),
        P("grp", "pts"),
        P(),
        P("grp", None),
        P("grp", None, None),
        P("grp", "pts"),
    )
    return jax.shard_map(
        functools.partial(shards, mesh.shape["pts"], mesh.shape["grp"]),
        mesh=mesh,
        in_specs=placed,
        out_specs=P("grp", None, "pts"),
        check_vma=False,
    )
```

```python
import functools
import math

import jax
import jax.numpy as jnp
import numpy as np
from jax import lax
from jax.experimental import pallas as pl
from jax.experimental.pallas import tpu as pltpu
from jax.sharding import PartitionSpec as P

NDIR = 36
NFREQ = 32
BLOCK = 128
QUAD = NDIR // 4
PIECE = 3
CUTS = ((0, 3, 9, 18, 27, 36), (0, 9, 18, 27, 33, 36))
LOADS = 4
HANDS = (
    (0, 0, 1),
    (1, 1, 2),
    (1, 1, 3),
    (1, 1, 0),
    (2, 2, 3),
    (2, 2, 1),
    (2, 2, 0),
    (3, 3, 2),
    (3, 3, 1),
    (3, 3, 0),
    (0, 1, 2),
    (0, 1, 3),
)
GREETED = (1, 3)
ARRIVALS = ((1, 2, 3), (0, 2, 3), (1, 3, 0), (2, 1, 0))
MESH = pl.DeviceIdType.MESH


def kernel(
    n_pts,
    n_grp,
    trig_ref,
    spec_hbm,
    coarse_hbm,
    east_hbm,
    north_hbm,
    turn_hbm,
    kern_hbm,
    mask_hbm,
    lists_hbm,
    blist_hbm,
    out_ref,
    spec_v,
    winds_v,
    kern_v,
    mask_v,
    lists_v,
    blist_s,
    trig_s,
    coarse_v,
    coarse_n,
    pick_v,
    own,
    prv,
    nxt,
    load_sem,
    spec_sem,
    co_send,
    co_recv,
    send_sem,
    recv_sem,
):
    pos = lax.axis_index("pts")
    grp = lax.axis_index("grp")
    after = lax.rem(pos + 1, n_pts)
    before = lax.rem(pos + n_pts - 1, n_pts)
    has_before = pos > 0
    has_after = pos < n_pts - 1
    group_points = mask_hbm.shape[1]
    ghosts = blist_hbm.shape[1]
    slots, comps = coarse_hbm.shape
    coarse_span = slots * n_pts

    barrier = pltpu.get_barrier_semaphore()

    @pl.when(has_before)
    def _():
        pl.semaphore_signal(barrier, inc=1, device_id={"pts": before}, device_id_type=MESH)

    @pl.when(has_after)
    def _():
        pl.semaphore_signal(barrier, inc=1, device_id={"pts": after}, device_id_type=MESH)

    for g in range(n_grp):
        for owner, sender, to in HANDS:
            if to == g and owner == sender:

                @pl.when(grp == to)
                def _():
                    pl.semaphore_signal(
                        barrier, inc=1, device_id={"grp": sender}, device_id_type=MESH
                    )

    here = pl.ds(pl.multiple_of(pos * BLOCK, BLOCK), BLOCK)
    rows = comps // LOADS
    spec_loads = [
        pltpu.make_async_copy(
            spec_hbm.at[pl.ds(i * rows, rows)], spec_v.at[pl.ds(i * rows, rows)], spec_sem.at[i]
        )
        for i in range(LOADS)
    ]
    early_loads = [
        pltpu.make_async_copy(trig_ref, trig_s, load_sem.at[0]),
        pltpu.make_async_copy(east_hbm, winds_v.at[0], load_sem.at[1]),
        pltpu.make_async_copy(north_hbm, winds_v.at[1], load_sem.at[2]),
        pltpu.make_async_copy(kern_hbm, kern_v, load_sem.at[3]),
        pltpu.make_async_copy(mask_hbm.at[:, here], mask_v, load_sem.at[4]),
        pltpu.make_async_copy(coarse_hbm, coarse_v.at[grp], load_sem.at[5]),
    ]
    late_loads = [
        pltpu.make_async_copy(lists_hbm.at[:, here], lists_v, load_sem.at[6]),
        pltpu.make_async_copy(blist_hbm, blist_s, load_sem.at[7]),
        pltpu.make_async_copy(turn_hbm, winds_v.at[2], load_sem.at[8]),
    ]
    for load in spec_loads + early_loads + late_loads:
        load.start()

    freq = lax.broadcasted_iota(jnp.int32, (NFREQ, BLOCK), 0).astype(jnp.float32)
    half_up = jnp.exp(freq * (0.5 * math.log(1.1)))
    courant = 0.65 * jnp.exp(freq * (-0.5 * math.log(1.1)))
    turn_factor = 0.5 + 0.5 * jnp.exp(freq * (-math.log(1.1)))

    for load in early_loads:
        load.wait()
    maskf = jnp.broadcast_to(mask_v[...].astype(jnp.float32), (NFREQ, BLOCK))
    east = jnp.broadcast_to(winds_v[0], (NFREQ, BLOCK))
    north = jnp.broadcast_to(winds_v[1], (NFREQ, BLOCK))
    kern_f = kern_v[...]
    kern_hi = kern_f.astype(jnp.bfloat16)
    kern_lo = (kern_f - kern_hi.astype(jnp.float32)).astype(jnp.bfloat16)
    kern = jnp.concatenate([kern_hi, kern_hi, kern_lo, kern_lo], axis=1)

    total = jnp.zeros((8, BLOCK), jnp.float32)
    for i in range(LOADS):
        spec_loads[i].wait()
        part = spec_v[i * rows : (i + 1) * rows, :].reshape(rows // 8, 8, BLOCK)
        total = total + jnp.sum(part, axis=0)
    etot = jnp.sum(total, axis=0, keepdims=True) * (1.0 / comps)
    diss = jnp.broadcast_to(0.3 * etot, (NFREQ, BLOCK)) * (0.5 + freq * (1.0 / NFREQ))

    def halo(step, c, way):
        first, end = CUTS[step][c], CUTS[step][c + 1]
        into = prv if way == 0 else nxt
        return pltpu.make_async_remote_copy(
            src_ref=own.at[step, pl.ds(first, end - first)],
            dst_ref=into.at[step, pl.ds(first, end - first)],
            send_sem=send_sem.at[step, way, c],
            recv_sem=recv_sem.at[step, way, c],
            device_id={"pts": after if way == 0 else before},
            device_id_type=MESH,
        )

    def send_both(step, c):
        @pl.when(has_after)
        def _():
            halo(step, c, 0).start()

        @pl.when(has_before)
        def _():
            halo(step, c, 1).start()

    def await_both(step, c):
        @pl.when(has_before)
        def _():
            halo(step, c, 0).wait_recv()

        @pl.when(has_after)
        def _():
            halo(step, c, 1).wait_recv()

    def sent_both(step, c):
        @pl.when(has_after)
        def _():
            halo(step, c, 0).wait_send()

        @pl.when(has_before)
        def _():
            halo(step, c, 1).wait_send()

    def hand(owner, to):
        own_block = coarse_v.at[owner]
        return pltpu.make_async_remote_copy(
            src_ref=own_block,
            dst_ref=own_block,
            send_sem=co_send.at[owner, to],
            recv_sem=co_recv.at[owner],
            device_id={"grp": to},
            device_id_type=MESH,
        )

    def source(first):
        cells = [spec_v[pl.ds(first + i, NFREQ, stride=NDIR), :] for i in range(PIECE)]
        wide = jnp.concatenate(cells, axis=1)
        wide_hi = wide.astype(jnp.bfloat16)
        wide_lo = (wide - wide_hi.astype(jnp.float32)).astype(jnp.bfloat16)
        mixed = jnp.dot(
            kern,
            jnp.concatenate([wide_hi, wide_lo, wide_hi, wide_lo], axis=0),
            preferred_element_type=jnp.float32,
        )
        for i in range(PIECE):
            d = first + i
            cell = cells[i]
            along = east * trig_s[0, d] + north * trig_s[1, d]
            grow = 0.1 * jnp.maximum(along * half_up - 1.0, 0.0)
            mix = mixed[:, i * BLOCK : (i + 1) * BLOCK]
            own[0, d] = maskf * (cell + cell * (grow - diss) + 0.2 * mix)

    parts = len(CUTS[0]) - 1
    for c in range(parts):
        for first in range(CUTS[0][c], CUTS[0][c + 1], PIECE):
            source(first)
        if c == 0:

            greeted = jnp.where(grp == 0, GREETED[0], GREETED[1])
            greeted += jnp.where(has_before, 1, 0) + jnp.where(has_after, 1, 0)
            pl.semaphore_wait(barrier, greeted)

            for g in range(n_grp):

                @pl.when(grp == g)
                def _():
                    for owner, sender, to in HANDS:
                        if owner == sender == g:
                            hand(owner, to).start()

        send_both(0, c)
    for load in late_loads:
        load.wait()
    lists = lists_v[...]
    shape = (4, BLOCK)
    slot = lists - (group_points + pos * ghosts)
    column = jnp.zeros(shape, jnp.int32)
    for k in range(ghosts):
        j = blist_s[0, k]
        col = lax.div(j, jnp.int32(coarse_span)) * slots + lax.rem(j, jnp.int32(slots))
        column = jnp.where(slot == k, col, column)
    rel = lists - (pos * BLOCK - BLOCK)
    is_far = lists >= group_points
    place = jnp.where(is_far, 3 * BLOCK + column, rel)

    window = lax.broadcasted_iota(jnp.int32, (4 * BLOCK, BLOCK), 0)
    for r in range(4):
        pick_v[r] = jnp.where(window == place[r : r + 1], 1.0, 0.0).astype(jnp.bfloat16)

    def clear(into):
        def clear_one(d, carry):
            for step in range(2):
                into[step, d] = jnp.zeros((NFREQ, BLOCK), jnp.float32)
            return carry

        lax.fori_loop(0, NDIR, clear_one, 0)

    @pl.when(pos == 0)
    def _():
        clear(prv)

    @pl.when(pos == n_pts - 1)
    def _():
        clear(nxt)

    for g in range(n_grp):

        @pl.when(grp == g)
        def _():
            for owner in ARRIVALS[g]:
                hand(owner, g).wait_recv()
                for relayed, sender, to in HANDS:
                    if relayed == owner and sender == g:
                        hand(owner, to).start()

    stacked = coarse_v[...].reshape(n_grp * slots, comps)
    pad = jnp.zeros((BLOCK - n_grp * slots, BLOCK), jnp.float32)
    for t in range(comps // BLOCK):
        tile = jnp.concatenate([stacked[:, t * BLOCK : (t + 1) * BLOCK], pad], axis=0)
        coarse_n[t * BLOCK : (t + 1) * BLOCK, :] = jnp.transpose(tile)

    def advect(step, first, end):
        quad = first // QUAD
        picks = jnp.concatenate(
            [pick_v[(quad + 1) // 2 % 2], pick_v[2 + quad // 2]], axis=1
        )
        cells = (end - first) * NFREQ
        windows = jnp.concatenate(
            [
                prv[step, first:end].reshape(cells, BLOCK),
                own[step, first:end].reshape(cells, BLOCK),
                nxt[step, first:end].reshape(cells, BLOCK),
                jnp.concatenate(
                    [coarse_n[pl.ds(d, NFREQ, stride=NDIR), :] for d in range(first, end)],
                    axis=0,
                ),
            ],
            axis=1,
        )
        high = windows.astype(jnp.bfloat16)
        low = (windows - high.astype(jnp.float32)).astype(jnp.bfloat16)
        both = jnp.dot(
            jnp.concatenate([high, low], axis=0), picks, preferred_element_type=jnp.float32
        )
        found = both[:cells] + both[cells:]
        for d in range(first, end):
            cell = own[step, d]
            at = (d - first) * NFREQ
            from_x = found[at : at + NFREQ, :BLOCK]
            from_y = found[at : at + NFREQ, BLOCK:]
            step_x = courant * trig_s[2, d]
            step_y = courant * trig_s[3, d]
            own[step + 1, d] = maskf * (
                cell - step_x * (cell - from_x) - step_y * (cell - from_y)
            )

    got = sent = 0
    for first in range(0, NDIR, QUAD):
        while got < parts and CUTS[0][got] < first + QUAD:
            await_both(0, got)
            got += 1
        advect(0, first, first + QUAD)
        while sent < parts and CUTS[1][sent + 1] <= first + QUAD:
            send_both(1, sent)
            sent += 1

    rate = jnp.broadcast_to(winds_v[2], (NFREQ, BLOCK)) * turn_factor
    slow = jnp.abs(rate)
    turning_up = rate > 0

    def refract(d):
        mine = own[2, d]
        up = jnp.where(turning_up, own[2, (d - 1) % NDIR], own[2, (d + 1) % NDIR])
        out_ref[pl.ds(d, NFREQ, stride=NDIR), :] = maskf * (mine - slow * (mine - up))

    done = 1
    for c in range(parts):
        await_both(1, c)
        advect(1, CUTS[1][c], CUTS[1][c + 1])
        while done < CUTS[1][c + 1] - 1:
            refract(done)
            done += 1
    refract(NDIR - 1)
    refract(0)

    for step in range(2):
        for c in range(parts):
            sent_both(step, c)
    for g in range(n_grp):

        @pl.when(grp == g)
        def _():
            for owner, sender, to in HANDS:
                if sender == g:
                    hand(owner, to).wait_send()


def trig_table():
    theta = 2.0 * math.pi * (np.arange(NDIR) + 0.5) / NDIR
    rows = [np.cos(theta), np.sin(theta), np.abs(np.cos(theta)), np.abs(np.sin(theta))]
    return np.stack(rows).astype(np.float32)


def shards(
    n_pts,
    n_grp,
    spectrum,
    coarse_spectra,
    wind_east,
    wind_north,
    refraction,
    freq_kernel,
    sea_mask,
    upwind_lists,
    boundary_list,
):
    comps = spectrum.shape[1]
    slots = coarse_spectra.shape[2]
    ghosts = boundary_list.shape[1]
    anyspace = pl.BlockSpec(memory_space=pl.ANY)
    block = (NDIR, NFREQ, BLOCK)
    out = pl.pallas_call(
        functools.partial(kernel, n_pts, n_grp),
        out_shape=jax.ShapeDtypeStruct((comps, BLOCK), jnp.float32),
        in_specs=[anyspace] * 10,
        out_specs=pl.BlockSpec(memory_space=pltpu.VMEM),
        scratch_shapes=[
            pltpu.VMEM((comps, BLOCK), jnp.float32),
            pltpu.VMEM((3, 1, BLOCK), jnp.float32),
            pltpu.VMEM((NFREQ, NFREQ), jnp.float32),
            pltpu.VMEM((1, BLOCK), jnp.int32),
            pltpu.VMEM((4, BLOCK), jnp.int32),
            pltpu.SMEM((1, ghosts), jnp.int32),
            pltpu.SMEM((4, NDIR), jnp.float32),
            pltpu.VMEM((n_grp, slots, comps), jnp.float32),
            pltpu.VMEM((comps, BLOCK), jnp.float32),
            pltpu.VMEM((4, 4 * BLOCK, BLOCK), jnp.bfloat16),
            pltpu.VMEM((3,) + block, jnp.float32),
            pltpu.VMEM((2,) + block, jnp.float32),
            pltpu.VMEM((2,) + block, jnp.float32),
            pltpu.SemaphoreType.DMA((9,)),
            pltpu.SemaphoreType.DMA((LOADS,)),
            pltpu.SemaphoreType.DMA((n_grp, n_grp)),
            pltpu.SemaphoreType.DMA((n_grp,)),
            pltpu.SemaphoreType.DMA((2, 2, len(CUTS[0]) - 1)),
            pltpu.SemaphoreType.DMA((2, 2, len(CUTS[0]) - 1)),
        ],
        compiler_params=pltpu.CompilerParams(
            collective_id=0, has_side_effects=True, vmem_limit_bytes=24 * 1024 * 1024
        ),
        name="wave_step",
    )(*[pltpu.with_memory_space_constraint(a, pltpu.HBM) for a in (
        jnp.asarray(trig_table()),
        spectrum[0],
        jnp.transpose(coarse_spectra[0]),
        wind_east,
        wind_north,
        refraction,
        freq_kernel,
        sea_mask,
        upwind_lists[0],
        boundary_list,
    )])
    return out[None]


def solution(mesh):
    placed = (
        P("grp", None, "pts"),
        P("grp", None, "pts"),
        P("grp", "pts"),
        P("grp", "pts"),
        P("grp", "pts"),
        P(),
        P("grp", None),
        P("grp", None, None),
        P("grp", "pts"),
    )
    return jax.shard_map(
        functools.partial(shards, mesh.shape["pts"], mesh.shape["grp"]),
        mesh=mesh,
        in_specs=placed,
        out_specs=P("grp", None, "pts"),
        check_vma=False,
    )
```

```python
import functools
import math

import jax
import jax.numpy as jnp
import numpy as np
from jax import lax
from jax.experimental import pallas as pl
from jax.experimental.pallas import tpu as pltpu
from jax.sharding import PartitionSpec as P

NDIR = 36
NFREQ = 32
BLOCK = 128
QUAD = NDIR // 4
PIECE = 3
CUTS = ((0, 3, 9, 18, 27, 36), (0, 9, 18, 27, 33, 36))
LOADS = 4
EAGER = 2
MESH = pl.DeviceIdType.MESH


def kernel(
    n_pts,
    n_grp,
    trig_ref,
    spec_hbm,
    coarse_hbm,
    east_hbm,
    north_hbm,
    turn_hbm,
    kern_hbm,
    mask_hbm,
    lists_hbm,
    blist_hbm,
    out_ref,
    spec_v,
    winds_v,
    kern_v,
    mask_v,
    lists_v,
    blist_s,
    trig_s,
    coarse_v,
    coarse_n,
    pick_v,
    own,
    prv,
    nxt,
    load_sem,
    spec_sem,
    hello,
    co_send,
    co_recv,
    send_sem,
    recv_sem,
):
    pos = lax.axis_index("pts")
    grp = lax.axis_index("grp")
    after = lax.rem(pos + 1, n_pts)
    before = lax.rem(pos + n_pts - 1, n_pts)
    has_before = pos > 0
    has_after = pos < n_pts - 1
    group_points = mask_hbm.shape[1]
    ghosts = blist_hbm.shape[1]
    slots, comps = coarse_hbm.shape
    coarse_span = slots * n_pts

    barrier = pltpu.get_barrier_semaphore()

    @pl.when(has_before)
    def _():
        pl.semaphore_signal(barrier, inc=1, device_id={"pts": before}, device_id_type=MESH)

    @pl.when(has_after)
    def _():
        pl.semaphore_signal(barrier, inc=1, device_id={"pts": after}, device_id_type=MESH)

    for k in range(1, n_grp):

        @pl.when(grp < k)
        def _():
            pl.semaphore_signal(barrier, inc=1, device_id={"grp": k}, device_id_type=MESH)

    here = pl.ds(pl.multiple_of(pos * BLOCK, BLOCK), BLOCK)
    rows = comps // LOADS
    spec_loads = [
        pltpu.make_async_copy(
            spec_hbm.at[pl.ds(i * rows, rows)], spec_v.at[pl.ds(i * rows, rows)], spec_sem.at[i]
        )
        for i in range(LOADS)
    ]
    early_loads = [
        pltpu.make_async_copy(trig_ref, trig_s, load_sem.at[0]),
        pltpu.make_async_copy(east_hbm, winds_v.at[0], load_sem.at[1]),
        pltpu.make_async_copy(north_hbm, winds_v.at[1], load_sem.at[2]),
        pltpu.make_async_copy(kern_hbm, kern_v, load_sem.at[3]),
        pltpu.make_async_copy(mask_hbm.at[:, here], mask_v, load_sem.at[4]),
    ]
    late_loads = [
        pltpu.make_async_copy(coarse_hbm, coarse_v.at[grp], load_sem.at[5]),
        pltpu.make_async_copy(lists_hbm.at[:, here], lists_v, load_sem.at[6]),
        pltpu.make_async_copy(blist_hbm, blist_s, load_sem.at[7]),
        pltpu.make_async_copy(turn_hbm, winds_v.at[2], load_sem.at[8]),
    ]
    for load in spec_loads + early_loads + late_loads:
        load.start()

    def hand(to):
        return pltpu.make_async_remote_copy(
            src_ref=coarse_hbm,
            dst_ref=coarse_v.at[grp],
            send_sem=co_send.at[to],
            recv_sem=co_recv.at[grp],
            device_id={"grp": to},
            device_id_type=MESH,
        )

    def arrival(owner):
        return pltpu.make_async_remote_copy(
            src_ref=coarse_v.at[owner],
            dst_ref=coarse_v.at[owner],
            send_sem=co_send.at[owner],
            recv_sem=co_recv.at[owner],
            device_id={"grp": owner},
            device_id_type=MESH,
        )

    def meet():
        greeted = grp + jnp.where(has_before, 1, 0) + jnp.where(has_after, 1, 0)
        pl.semaphore_wait(barrier, greeted)
        for k in range(n_grp - 1):

            @pl.when(grp > k)
            def _():
                pl.semaphore_signal(
                    hello.at[grp], inc=1, device_id={"grp": k}, device_id_type=MESH
                )

        for k in range(n_grp - 1):

            @pl.when((grp > k) & ((k != 0) | (grp != 2)))
            def _():
                hand(k).start()

    @pl.when(grp >= EAGER)
    def _():
        meet()

    freq = lax.broadcasted_iota(jnp.int32, (NFREQ, BLOCK), 0).astype(jnp.float32)
    half_up = jnp.exp(freq * (0.5 * math.log(1.1)))
    courant = 0.65 * jnp.exp(freq * (-0.5 * math.log(1.1)))
    turn_factor = 0.5 + 0.5 * jnp.exp(freq * (-math.log(1.1)))

    for load in early_loads:
        load.wait()
    maskf = jnp.broadcast_to(mask_v[...].astype(jnp.float32), (NFREQ, BLOCK))
    east = jnp.broadcast_to(winds_v[0], (NFREQ, BLOCK))
    north = jnp.broadcast_to(winds_v[1], (NFREQ, BLOCK))
    kern_f = kern_v[...]
    kern_hi = kern_f.astype(jnp.bfloat16)
    kern_lo = (kern_f - kern_hi.astype(jnp.float32)).astype(jnp.bfloat16)
    kern = jnp.concatenate([kern_hi, kern_hi, kern_lo, kern_lo], axis=1)

    total = jnp.zeros((8, BLOCK), jnp.float32)
    for i in range(LOADS):
        spec_loads[i].wait()
        part = spec_v[i * rows : (i + 1) * rows, :].reshape(rows // 8, 8, BLOCK)
        total = total + jnp.sum(part, axis=0)
    etot = jnp.sum(total, axis=0, keepdims=True) * (1.0 / comps)
    diss = jnp.broadcast_to(0.3 * etot, (NFREQ, BLOCK)) * (0.5 + freq * (1.0 / NFREQ))

    def halo(step, c, way):
        first, end = CUTS[step][c], CUTS[step][c + 1]
        into = prv if way == 0 else nxt
        return pltpu.make_async_remote_copy(
            src_ref=own.at[step, pl.ds(first, end - first)],
            dst_ref=into.at[step, pl.ds(first, end - first)],
            send_sem=send_sem.at[step, way, c],
            recv_sem=recv_sem.at[step, way, c],
            device_id={"pts": after if way == 0 else before},
            device_id_type=MESH,
        )

    def send_both(step, c):
        @pl.when(has_after)
        def _():
            halo(step, c, 0).start()

        @pl.when(has_before)
        def _():
            halo(step, c, 1).start()

    def await_both(step, c):
        @pl.when(has_before)
        def _():
            halo(step, c, 0).wait_recv()

        @pl.when(has_after)
        def _():
            halo(step, c, 1).wait_recv()

    def sent_both(step, c):
        @pl.when(has_after)
        def _():
            halo(step, c, 0).wait_send()

        @pl.when(has_before)
        def _():
            halo(step, c, 1).wait_send()

    def source(first):
        cells = [spec_v[pl.ds(first + i, NFREQ, stride=NDIR), :] for i in range(PIECE)]
        wide = jnp.concatenate(cells, axis=1)
        wide_hi = wide.astype(jnp.bfloat16)
        wide_lo = (wide - wide_hi.astype(jnp.float32)).astype(jnp.bfloat16)
        mixed = jnp.dot(
            kern,
            jnp.concatenate([wide_hi, wide_lo, wide_hi, wide_lo], axis=0),
            preferred_element_type=jnp.float32,
        )
        for i in range(PIECE):
            d = first + i
            cell = cells[i]
            along = east * trig_s[0, d] + north * trig_s[1, d]
            grow = 0.1 * jnp.maximum(along * half_up - 1.0, 0.0)
            mix = mixed[:, i * BLOCK : (i + 1) * BLOCK]
            own[0, d] = maskf * (cell + cell * (grow - diss) + 0.2 * mix)

    parts = len(CUTS[0]) - 1
    for c in range(parts):
        for first in range(CUTS[0][c], CUTS[0][c + 1], PIECE):
            source(first)
        if c == 0:

            @pl.when(grp < EAGER)
            def _():
                meet()

        send_both(0, c)
    @pl.when(grp == 2)
    def _():
        hand(0).start()

    for k in range(1, n_grp):

        @pl.when(grp < k)
        def _():
            pl.semaphore_wait(hello.at[k], 1)
            hand(k).start()

    for load in late_loads:
        load.wait()
    lists = lists_v[...]
    shape = (4, BLOCK)
    slot = lists - (group_points + pos * ghosts)
    column = jnp.zeros(shape, jnp.int32)
    for k in range(ghosts):
        j = blist_s[0, k]
        col = lax.div(j, jnp.int32(coarse_span)) * slots + lax.rem(j, jnp.int32(slots))
        column = jnp.where(slot == k, col, column)
    rel = lists - (pos * BLOCK - BLOCK)
    is_far = lists >= group_points
    place = jnp.where(is_far, 3 * BLOCK + column, rel)

    window = lax.broadcasted_iota(jnp.int32, (4 * BLOCK, BLOCK), 0)
    for r in range(4):
        pick_v[r] = jnp.where(window == place[r : r + 1], 1.0, 0.0).astype(jnp.bfloat16)

    def clear(into):
        def clear_one(d, carry):
            for step in range(2):
                into[step, d] = jnp.zeros((NFREQ, BLOCK), jnp.float32)
            return carry

        lax.fori_loop(0, NDIR, clear_one, 0)

    @pl.when(pos == 0)
    def _():
        clear(prv)

    @pl.when(pos == n_pts - 1)
    def _():
        clear(nxt)

    for k in range(n_grp):

        @pl.when(grp != k)
        def _():
            arrival(k).wait_recv()

    stacked = coarse_v[...].reshape(n_grp * slots, comps)
    pad = jnp.zeros((BLOCK - n_grp * slots, BLOCK), jnp.float32)
    for t in range(comps // BLOCK):
        tile = jnp.concatenate([stacked[:, t * BLOCK : (t + 1) * BLOCK], pad], axis=0)
        coarse_n[t * BLOCK : (t + 1) * BLOCK, :] = jnp.transpose(tile)

    def advect(step, first, end):
        quad = first // QUAD
        picks = jnp.concatenate(
            [pick_v[(quad + 1) // 2 % 2], pick_v[2 + quad // 2]], axis=1
        )
        cells = (end - first) * NFREQ
        windows = jnp.concatenate(
            [
                prv[step, first:end].reshape(cells, BLOCK),
                own[step, first:end].reshape(cells, BLOCK),
                nxt[step, first:end].reshape(cells, BLOCK),
                jnp.concatenate(
                    [coarse_n[pl.ds(d, NFREQ, stride=NDIR), :] for d in range(first, end)],
                    axis=0,
                ),
            ],
            axis=1,
        )
        high = windows.astype(jnp.bfloat16)
        low = (windows - high.astype(jnp.float32)).astype(jnp.bfloat16)
        both = jnp.dot(
            jnp.concatenate([high, low], axis=0), picks, preferred_element_type=jnp.float32
        )
        found = both[:cells] + both[cells:]
        for d in range(first, end):
            cell = own[step, d]
            at = (d - first) * NFREQ
            from_x = found[at : at + NFREQ, :BLOCK]
            from_y = found[at : at + NFREQ, BLOCK:]
            step_x = courant * trig_s[2, d]
            step_y = courant * trig_s[3, d]
            own[step + 1, d] = maskf * (
                cell - step_x * (cell - from_x) - step_y * (cell - from_y)
            )

    got = sent = 0
    for first in range(0, NDIR, QUAD):
        while got < parts and CUTS[0][got] < first + QUAD:
            await_both(0, got)
            got += 1
        advect(0, first, first + QUAD)
        while sent < parts and CUTS[1][sent + 1] <= first + QUAD:
            send_both(1, sent)
            sent += 1

    rate = jnp.broadcast_to(winds_v[2], (NFREQ, BLOCK)) * turn_factor
    slow = jnp.abs(rate)
    turning_up = rate > 0

    def refract(d):
        mine = own[2, d]
        up = jnp.where(turning_up, own[2, (d - 1) % NDIR], own[2, (d + 1) % NDIR])
        out_ref[pl.ds(d, NFREQ, stride=NDIR), :] = maskf * (mine - slow * (mine - up))

    done = 1
    for c in range(parts):
        await_both(1, c)
        advect(1, CUTS[1][c], CUTS[1][c + 1])
        while done < CUTS[1][c + 1] - 1:
            refract(done)
            done += 1
    refract(NDIR - 1)
    refract(0)

    for step in range(2):
        for c in range(parts):
            sent_both(step, c)
    for k in range(n_grp):

        @pl.when(grp != k)
        def _():
            hand(k).wait_send()


def trig_table():
    theta = 2.0 * math.pi * (np.arange(NDIR) + 0.5) / NDIR
    rows = [np.cos(theta), np.sin(theta), np.abs(np.cos(theta)), np.abs(np.sin(theta))]
    return np.stack(rows).astype(np.float32)


def shards(
    n_pts,
    n_grp,
    spectrum,
    coarse_spectra,
    wind_east,
    wind_north,
    refraction,
    freq_kernel,
    sea_mask,
    upwind_lists,
    boundary_list,
):
    comps = spectrum.shape[1]
    slots = coarse_spectra.shape[2]
    ghosts = boundary_list.shape[1]
    anyspace = pl.BlockSpec(memory_space=pl.ANY)
    block = (NDIR, NFREQ, BLOCK)
    out = pl.pallas_call(
        functools.partial(kernel, n_pts, n_grp),
        out_shape=jax.ShapeDtypeStruct((comps, BLOCK), jnp.float32),
        in_specs=[anyspace] * 10,
        out_specs=pl.BlockSpec(memory_space=pltpu.VMEM),
        scratch_shapes=[
            pltpu.VMEM((comps, BLOCK), jnp.float32),
            pltpu.VMEM((3, 1, BLOCK), jnp.float32),
            pltpu.VMEM((NFREQ, NFREQ), jnp.float32),
            pltpu.VMEM((1, BLOCK), jnp.int32),
            pltpu.VMEM((4, BLOCK), jnp.int32),
            pltpu.SMEM((1, ghosts), jnp.int32),
            pltpu.SMEM((4, NDIR), jnp.float32),
            pltpu.VMEM((n_grp, slots, comps), jnp.float32),
            pltpu.VMEM((comps, BLOCK), jnp.float32),
            pltpu.VMEM((4, 4 * BLOCK, BLOCK), jnp.bfloat16),
            pltpu.VMEM((3,) + block, jnp.float32),
            pltpu.VMEM((2,) + block, jnp.float32),
            pltpu.VMEM((2,) + block, jnp.float32),
            pltpu.SemaphoreType.DMA((9,)),
            pltpu.SemaphoreType.DMA((LOADS,)),
            pltpu.SemaphoreType.REGULAR((n_grp,)),
            pltpu.SemaphoreType.DMA((n_grp,)),
            pltpu.SemaphoreType.DMA((n_grp,)),
            pltpu.SemaphoreType.DMA((2, 2, len(CUTS[0]) - 1)),
            pltpu.SemaphoreType.DMA((2, 2, len(CUTS[0]) - 1)),
        ],
        compiler_params=pltpu.CompilerParams(
            collective_id=0, has_side_effects=True, vmem_limit_bytes=24 * 1024 * 1024
        ),
        name="wave_step",
    )(*[pltpu.with_memory_space_constraint(a, pltpu.HBM) for a in (
        jnp.asarray(trig_table()),
        spectrum[0],
        jnp.transpose(coarse_spectra[0]),
        wind_east,
        wind_north,
        refraction,
        freq_kernel,
        sea_mask,
        upwind_lists[0],
        boundary_list,
    )])
    return out[None]


def solution(mesh):
    placed = (
        P("grp", None, "pts"),
        P("grp", None, "pts"),
        P("grp", "pts"),
        P("grp", "pts"),
        P("grp", "pts"),
        P(),
        P("grp", None),
        P("grp", None, None),
        P("grp", "pts"),
    )
    return jax.shard_map(
        functools.partial(shards, mesh.shape["pts"], mesh.shape["grp"]),
        mesh=mesh,
        in_specs=placed,
        out_specs=P("grp", None, "pts"),
        check_vma=False,
    )
```

```python
import functools
import math

import jax
import jax.numpy as jnp
import numpy as np
from jax import lax
from jax.experimental import pallas as pl
from jax.experimental.pallas import tpu as pltpu
from jax.sharding import PartitionSpec as P

NDIR = 36
NFREQ = 32
BLOCK = 128
QUAD = NDIR // 4
PIECE = 3
CUTS = ((0, 3, 9, 18, 27, 36), (0, 9, 18, 27, 33, 36))
EARLY = ()
LOADS = 2
EAGER = 2
MESH = pl.DeviceIdType.MESH


def kernel(
    n_pts,
    n_grp,
    trig_ref,
    spec_hbm,
    coarse_hbm,
    east_hbm,
    north_hbm,
    turn_hbm,
    kern_hbm,
    mask_hbm,
    lists_hbm,
    blist_hbm,
    out_ref,
    spec_v,
    winds_v,
    kern_v,
    mask_v,
    lists_v,
    blist_s,
    trig_s,
    coarse_v,
    coarse_n,
    pick_v,
    own,
    prv,
    nxt,
    load_sem,
    spec_sem,
    hello,
    co_send,
    co_recv,
    send_sem,
    recv_sem,
):
    pos = lax.axis_index("pts")
    grp = lax.axis_index("grp")
    after = lax.rem(pos + 1, n_pts)
    before = lax.rem(pos + n_pts - 1, n_pts)
    has_before = pos > 0
    has_after = pos < n_pts - 1
    group_points = mask_hbm.shape[1]
    ghosts = blist_hbm.shape[1]
    slots, comps = coarse_hbm.shape
    coarse_span = slots * n_pts

    barrier = pltpu.get_barrier_semaphore()

    @pl.when(has_before)
    def _():
        pl.semaphore_signal(barrier, inc=1, device_id={"pts": before}, device_id_type=MESH)

    @pl.when(has_after)
    def _():
        pl.semaphore_signal(barrier, inc=1, device_id={"pts": after}, device_id_type=MESH)

    for k in range(1, n_grp):

        @pl.when(grp < k)
        def _():
            pl.semaphore_signal(barrier, inc=1, device_id={"grp": k}, device_id_type=MESH)

    here = pl.ds(pl.multiple_of(pos * BLOCK, BLOCK), BLOCK)
    rows = comps // LOADS
    spec_loads = [
        pltpu.make_async_copy(
            spec_hbm.at[pl.ds(i * rows, rows)], spec_v.at[pl.ds(i * rows, rows)], spec_sem.at[i]
        )
        for i in range(LOADS)
    ]
    early_loads = [
        pltpu.make_async_copy(trig_ref, trig_s, load_sem.at[0]),
        pltpu.make_async_copy(east_hbm, winds_v.at[0], load_sem.at[1]),
        pltpu.make_async_copy(north_hbm, winds_v.at[1], load_sem.at[2]),
        pltpu.make_async_copy(kern_hbm, kern_v, load_sem.at[3]),
        pltpu.make_async_copy(mask_hbm.at[:, here], mask_v, load_sem.at[4]),
    ]
    late_loads = [
        pltpu.make_async_copy(coarse_hbm, coarse_v.at[grp], load_sem.at[5]),
        pltpu.make_async_copy(lists_hbm.at[:, here], lists_v, load_sem.at[6]),
        pltpu.make_async_copy(blist_hbm, blist_s, load_sem.at[7]),
        pltpu.make_async_copy(turn_hbm, winds_v.at[2], load_sem.at[8]),
    ]
    for load in spec_loads + early_loads + late_loads:
        load.start()

    def hand(to):
        return pltpu.make_async_remote_copy(
            src_ref=coarse_hbm,
            dst_ref=coarse_v.at[grp],
            send_sem=co_send.at[to],
            recv_sem=co_recv.at[grp],
            device_id={"grp": to},
            device_id_type=MESH,
        )

    def arrival(owner):
        return pltpu.make_async_remote_copy(
            src_ref=coarse_v.at[owner],
            dst_ref=coarse_v.at[owner],
            send_sem=co_send.at[owner],
            recv_sem=co_recv.at[owner],
            device_id={"grp": owner},
            device_id_type=MESH,
        )

    def meet():
        greeted = grp + jnp.where(has_before, 1, 0) + jnp.where(has_after, 1, 0)
        pl.semaphore_wait(barrier, greeted)
        for k in range(n_grp - 1):

            @pl.when(grp > k)
            def _():
                pl.semaphore_signal(
                    hello.at[grp], inc=1, device_id={"grp": k}, device_id_type=MESH
                )

        for k in range(n_grp - 1):

            @pl.when((grp > k) & ((k != 0) | (grp != 2)))
            def _():
                hand(k).start()

    @pl.when(grp >= EAGER)
    def _():
        meet()

    freq = lax.broadcasted_iota(jnp.int32, (NFREQ, BLOCK), 0).astype(jnp.float32)
    half_up = jnp.exp(freq * (0.5 * math.log(1.1)))
    courant = 0.65 * jnp.exp(freq * (-0.5 * math.log(1.1)))
    turn_factor = 0.5 + 0.5 * jnp.exp(freq * (-math.log(1.1)))

    for load in early_loads:
        load.wait()
    maskf = jnp.broadcast_to(mask_v[...].astype(jnp.float32), (NFREQ, BLOCK))
    east = jnp.broadcast_to(winds_v[0], (NFREQ, BLOCK))
    north = jnp.broadcast_to(winds_v[1], (NFREQ, BLOCK))
    kern_f = kern_v[...]
    kern_hi = kern_f.astype(jnp.bfloat16)
    kern_lo = (kern_f - kern_hi.astype(jnp.float32)).astype(jnp.bfloat16)
    kern = jnp.concatenate([kern_hi, kern_hi, kern_lo, kern_lo], axis=1)

    total = jnp.zeros((8, BLOCK), jnp.float32)
    for i in range(LOADS):
        spec_loads[i].wait()
        part = spec_v[i * rows : (i + 1) * rows, :].reshape(rows // 8, 8, BLOCK)
        total = total + jnp.sum(part, axis=0)
    etot = jnp.sum(total, axis=0, keepdims=True) * (1.0 / comps)
    diss = jnp.broadcast_to(0.3 * etot, (NFREQ, BLOCK)) * (0.5 + freq * (1.0 / NFREQ))

    def halo(step, c, way):
        first, end = CUTS[step][c], CUTS[step][c + 1]
        into = prv if way == 0 else nxt
        return pltpu.make_async_remote_copy(
            src_ref=own.at[step, pl.ds(first, end - first)],
            dst_ref=into.at[step, pl.ds(first, end - first)],
            send_sem=send_sem.at[step, way, c],
            recv_sem=recv_sem.at[step, way, c],
            device_id={"pts": after if way == 0 else before},
            device_id_type=MESH,
        )

    def send_both(step, c):
        @pl.when(has_after)
        def _():
            halo(step, c, 0).start()

        @pl.when(has_before)
        def _():
            halo(step, c, 1).start()

    def await_both(step, c):
        @pl.when(has_before)
        def _():
            halo(step, c, 0).wait_recv()

        @pl.when(has_after)
        def _():
            halo(step, c, 1).wait_recv()

    def drain(copies):
        @pl.when(has_after)
        def _():
            for step, c in copies:
                halo(step, c, 0).wait_send()

        @pl.when(has_before)
        def _():
            for step, c in copies:
                halo(step, c, 1).wait_send()

    def source(first):
        cells = [spec_v[pl.ds(first + i, NFREQ, stride=NDIR), :] for i in range(PIECE)]
        wide = jnp.concatenate(cells, axis=1)
        wide_hi = wide.astype(jnp.bfloat16)
        wide_lo = (wide - wide_hi.astype(jnp.float32)).astype(jnp.bfloat16)
        mixed = jnp.dot(
            kern,
            jnp.concatenate([wide_hi, wide_lo, wide_hi, wide_lo], axis=0),
            preferred_element_type=jnp.float32,
        )
        for i in range(PIECE):
            d = first + i
            cell = cells[i]
            along = east * trig_s[0, d] + north * trig_s[1, d]
            grow = 0.1 * jnp.maximum(along * half_up - 1.0, 0.0)
            mix = mixed[:, i * BLOCK : (i + 1) * BLOCK]
            own[0, d] = maskf * (cell + cell * (grow - diss) + 0.2 * mix)

    parts = [len(cuts) - 1 for cuts in CUTS]
    for c in range(parts[0]):
        for first in range(CUTS[0][c], CUTS[0][c + 1], PIECE):
            source(first)
        if c == 0:

            @pl.when(grp < EAGER)
            def _():
                meet()

        send_both(0, c)
    @pl.when(grp == 2)
    def _():
        hand(0).start()

    for k in range(1, n_grp):

        @pl.when(grp < k)
        def _():
            pl.semaphore_wait(hello.at[k], 1)
            hand(k).start()

    for load in late_loads:
        load.wait()
    lists = lists_v[...]
    shape = (4, BLOCK)
    slot = lists - (group_points + pos * ghosts)
    column = jnp.zeros(shape, jnp.int32)
    for k in range(ghosts):
        j = blist_s[0, k]
        col = lax.div(j, jnp.int32(coarse_span)) * slots + lax.rem(j, jnp.int32(slots))
        column = jnp.where(slot == k, col, column)
    rel = lists - (pos * BLOCK - BLOCK)
    is_far = lists >= group_points
    place = jnp.where(is_far, 3 * BLOCK + column, rel)

    window = lax.broadcasted_iota(jnp.int32, (4 * BLOCK, BLOCK), 0)
    for r in range(4):
        pick_v[r] = jnp.where(window == place[r : r + 1], 1.0, 0.0).astype(jnp.bfloat16)

    coarse_n[...] = jnp.zeros((comps, BLOCK), jnp.float32)

    def clear(into):
        def clear_one(d, carry):
            for step in range(2):
                into[step, d] = jnp.zeros((NFREQ, BLOCK), jnp.float32)
            return carry

        lax.fori_loop(0, NDIR, clear_one, 0)

    @pl.when(pos == 0)
    def _():
        clear(prv)

    @pl.when(pos == n_pts - 1)
    def _():
        clear(nxt)

    for k in range(n_grp):

        @pl.when(grp != k)
        def _():
            arrival(k).wait_recv()

    stacked = coarse_v[...].reshape(n_grp * slots, comps)
    for t in range(comps // BLOCK):
        tile = stacked[:, t * BLOCK : (t + 1) * BLOCK]
        coarse_n[t * BLOCK : (t + 1) * BLOCK, : n_grp * slots] = jnp.transpose(tile)

    def advect(step, first, end):
        quad = first // QUAD
        picks = jnp.concatenate(
            [pick_v[(quad + 1) // 2 % 2], pick_v[2 + quad // 2]], axis=1
        )
        cells = (end - first) * NFREQ
        windows = jnp.concatenate(
            [
                prv[step, first:end].reshape(cells, BLOCK),
                own[step, first:end].reshape(cells, BLOCK),
                nxt[step, first:end].reshape(cells, BLOCK),
                jnp.concatenate(
                    [coarse_n[pl.ds(d, NFREQ, stride=NDIR), :] for d in range(first, end)],
                    axis=0,
                ),
            ],
            axis=1,
        )
        high = windows.astype(jnp.bfloat16)
        low = (windows - high.astype(jnp.float32)).astype(jnp.bfloat16)
        both = jnp.dot(
            jnp.concatenate([high, low], axis=0), picks, preferred_element_type=jnp.float32
        )
        found = both[:cells] + both[cells:]
        for d in range(first, end):
            cell = own[step, d]
            at = (d - first) * NFREQ
            from_x = found[at : at + NFREQ, :BLOCK]
            from_y = found[at : at + NFREQ, BLOCK:]
            step_x = courant * trig_s[2, d]
            step_y = courant * trig_s[3, d]
            own[step + 1, d] = maskf * (
                cell - step_x * (cell - from_x) - step_y * (cell - from_y)
            )

    got = sent = 0
    edges = sorted({*range(0, NDIR + 1, QUAD), *EARLY})
    for first, end in zip(edges, edges[1:]):
        while got < parts[0] and CUTS[0][got] < end:
            await_both(0, got)
            got += 1
        advect(0, first, end)
        while sent < parts[1] and CUTS[1][sent + 1] <= end:
            send_both(1, sent)
            sent += 1

    rate = jnp.broadcast_to(winds_v[2], (NFREQ, BLOCK)) * turn_factor
    slow = jnp.abs(rate)
    turning_up = rate > 0

    def refract(d):
        mine = own[2, d]
        up = jnp.where(turning_up, own[2, (d - 1) % NDIR], own[2, (d + 1) % NDIR])
        out_ref[pl.ds(d, NFREQ, stride=NDIR), :] = maskf * (mine - slow * (mine - up))

    done = 1
    for c in range(parts[1]):
        if c == parts[1] - 1:
            drain([(0, k) for k in range(parts[0])] + [(1, k) for k in range(c)])
            for k in range(n_grp):

                @pl.when(grp != k)
                def _():
                    hand(k).wait_send()

        await_both(1, c)
        advect(1, CUTS[1][c], CUTS[1][c + 1])
        while done < CUTS[1][c + 1] - 1:
            refract(done)
            done += 1
    refract(NDIR - 1)
    refract(0)

    drain([(1, parts[1] - 1)])


def trig_table():
    theta = 2.0 * math.pi * (np.arange(NDIR) + 0.5) / NDIR
    rows = [np.cos(theta), np.sin(theta), np.abs(np.cos(theta)), np.abs(np.sin(theta))]
    return np.stack(rows).astype(np.float32)


def shards(
    n_pts,
    n_grp,
    spectrum,
    coarse_spectra,
    wind_east,
    wind_north,
    refraction,
    freq_kernel,
    sea_mask,
    upwind_lists,
    boundary_list,
):
    comps = spectrum.shape[1]
    slots = coarse_spectra.shape[2]
    ghosts = boundary_list.shape[1]
    anyspace = pl.BlockSpec(memory_space=pl.ANY)
    block = (NDIR, NFREQ, BLOCK)
    out = pl.pallas_call(
        functools.partial(kernel, n_pts, n_grp),
        out_shape=jax.ShapeDtypeStruct((comps, BLOCK), jnp.float32),
        in_specs=[anyspace] * 10,
        out_specs=pl.BlockSpec(memory_space=pltpu.VMEM),
        scratch_shapes=[
            pltpu.VMEM((comps, BLOCK), jnp.float32),
            pltpu.VMEM((3, 1, BLOCK), jnp.float32),
            pltpu.VMEM((NFREQ, NFREQ), jnp.float32),
            pltpu.VMEM((1, BLOCK), jnp.int32),
            pltpu.VMEM((4, BLOCK), jnp.int32),
            pltpu.SMEM((1, ghosts), jnp.int32),
            pltpu.SMEM((4, NDIR), jnp.float32),
            pltpu.VMEM((n_grp, slots, comps), jnp.float32),
            pltpu.VMEM((comps, BLOCK), jnp.float32),
            pltpu.VMEM((4, 4 * BLOCK, BLOCK), jnp.bfloat16),
            pltpu.VMEM((3,) + block, jnp.float32),
            pltpu.VMEM((2,) + block, jnp.float32),
            pltpu.VMEM((2,) + block, jnp.float32),
            pltpu.SemaphoreType.DMA((9,)),
            pltpu.SemaphoreType.DMA((LOADS,)),
            pltpu.SemaphoreType.REGULAR((n_grp,)),
            pltpu.SemaphoreType.DMA((n_grp,)),
            pltpu.SemaphoreType.DMA((n_grp,)),
            pltpu.SemaphoreType.DMA((2, 2, max(map(len, CUTS)) - 1)),
            pltpu.SemaphoreType.DMA((2, 2, max(map(len, CUTS)) - 1)),
        ],
        compiler_params=pltpu.CompilerParams(
            collective_id=0, has_side_effects=True, vmem_limit_bytes=24 * 1024 * 1024
        ),
        name="wave_step",
    )(*[pltpu.with_memory_space_constraint(a, pltpu.HBM) for a in (
        jnp.asarray(trig_table()),
        spectrum[0],
        jnp.transpose(coarse_spectra[0]),
        wind_east,
        wind_north,
        refraction,
        freq_kernel,
        sea_mask,
        upwind_lists[0],
        boundary_list,
    )])
    return out[None]


def solution(mesh):
    placed = (
        P("grp", None, "pts"),
        P("grp", None, "pts"),
        P("grp", "pts"),
        P("grp", "pts"),
        P("grp", "pts"),
        P(),
        P("grp", None),
        P("grp", None, None),
        P("grp", "pts"),
    )
    return jax.shard_map(
        functools.partial(shards, mesh.shape["pts"], mesh.shape["grp"]),
        mesh=mesh,
        in_specs=placed,
        out_specs=P("grp", None, "pts"),
        check_vma=False,
    )
```

```python
import functools
import math

import jax
import jax.numpy as jnp
import numpy as np
from jax import lax
from jax.experimental import pallas as pl
from jax.experimental.pallas import tpu as pltpu
from jax.sharding import PartitionSpec as P

NDIR = 36
NFREQ = 32
BLOCK = 128
QUAD = NDIR // 4
PIECE = 3
CUTS = ((0, 3, 9, 18, 27, 36), (0, 9, 18, 27, 33, 36))
EARLY = ()
LOADS = 2
EAGER = 2
MESH = pl.DeviceIdType.MESH


def kernel(
    n_pts,
    n_grp,
    trig_ref,
    spec_hbm,
    coarse_hbm,
    east_hbm,
    north_hbm,
    turn_hbm,
    kern_hbm,
    mask_hbm,
    lists_hbm,
    blist_hbm,
    out_ref,
    spec_v,
    winds_v,
    kern_v,
    mask_v,
    lists_v,
    blist_s,
    trig_s,
    coarse_v,
    coarse_n,
    pick_v,
    own,
    prv,
    nxt,
    load_sem,
    spec_sem,
    hello,
    co_send,
    co_recv,
    send_sem,
    recv_sem,
):
    pos = lax.axis_index("pts")
    grp = lax.axis_index("grp")
    after = lax.rem(pos + 1, n_pts)
    before = lax.rem(pos + n_pts - 1, n_pts)
    has_before = pos > 0
    has_after = pos < n_pts - 1
    group_points = mask_hbm.shape[1]
    ghosts = blist_hbm.shape[1]
    slots, comps = coarse_hbm.shape
    coarse_span = slots * n_pts

    barrier = pltpu.get_barrier_semaphore()

    @pl.when(has_before)
    def _():
        pl.semaphore_signal(barrier, inc=1, device_id={"pts": before}, device_id_type=MESH)

    @pl.when(has_after)
    def _():
        pl.semaphore_signal(barrier, inc=1, device_id={"pts": after}, device_id_type=MESH)

    for k in range(1, n_grp):

        @pl.when(grp < k)
        def _():
            pl.semaphore_signal(barrier, inc=1, device_id={"grp": k}, device_id_type=MESH)

    here = pl.ds(pl.multiple_of(pos * BLOCK, BLOCK), BLOCK)
    rows = comps // LOADS
    spec_loads = [
        pltpu.make_async_copy(
            spec_hbm.at[pl.ds(i * rows, rows)], spec_v.at[pl.ds(i * rows, rows)], spec_sem.at[i]
        )
        for i in range(LOADS)
    ]
    early_loads = [
        pltpu.make_async_copy(trig_ref, trig_s, load_sem.at[0]),
        pltpu.make_async_copy(east_hbm, winds_v.at[0], load_sem.at[1]),
        pltpu.make_async_copy(north_hbm, winds_v.at[1], load_sem.at[2]),
        pltpu.make_async_copy(kern_hbm, kern_v, load_sem.at[3]),
        pltpu.make_async_copy(mask_hbm.at[:, here], mask_v, load_sem.at[4]),
    ]
    late_loads = [
        pltpu.make_async_copy(coarse_hbm, coarse_v.at[grp], load_sem.at[5]),
        pltpu.make_async_copy(lists_hbm.at[:, here], lists_v, load_sem.at[6]),
        pltpu.make_async_copy(blist_hbm, blist_s, load_sem.at[7]),
        pltpu.make_async_copy(turn_hbm, winds_v.at[2], load_sem.at[8]),
    ]
    for load in spec_loads + early_loads + late_loads:
        load.start()

    def hand(to):
        return pltpu.make_async_remote_copy(
            src_ref=coarse_hbm,
            dst_ref=coarse_v.at[grp],
            send_sem=co_send.at[to],
            recv_sem=co_recv.at[grp],
            device_id={"grp": to},
            device_id_type=MESH,
        )

    def arrival(owner):
        return pltpu.make_async_remote_copy(
            src_ref=coarse_v.at[owner],
            dst_ref=coarse_v.at[owner],
            send_sem=co_send.at[owner],
            recv_sem=co_recv.at[owner],
            device_id={"grp": owner},
            device_id_type=MESH,
        )

    def meet():
        greeted = grp + jnp.where(has_before, 1, 0) + jnp.where(has_after, 1, 0)
        pl.semaphore_wait(barrier, greeted)
        for k in range(n_grp - 1):

            @pl.when(grp > k)
            def _():
                pl.semaphore_signal(
                    hello.at[grp], inc=1, device_id={"grp": k}, device_id_type=MESH
                )

        for k in range(n_grp - 1):

            @pl.when((grp > k) & ((k != 0) | (grp != 2)))
            def _():
                hand(k).start()

    @pl.when(grp >= EAGER)
    def _():
        meet()

    freq = lax.broadcasted_iota(jnp.int32, (NFREQ, BLOCK), 0).astype(jnp.float32)
    half_up = jnp.exp(freq * (0.5 * math.log(1.1)))
    courant = 0.65 * jnp.exp(freq * (-0.5 * math.log(1.1)))
    turn_factor = 0.5 + 0.5 * jnp.exp(freq * (-math.log(1.1)))

    for load in early_loads:
        load.wait()
    maskf = jnp.broadcast_to(mask_v[...].astype(jnp.float32), (NFREQ, BLOCK))
    east = jnp.broadcast_to(winds_v[0], (NFREQ, BLOCK))
    north = jnp.broadcast_to(winds_v[1], (NFREQ, BLOCK))
    kern_f = kern_v[...]
    kern_hi = kern_f.astype(jnp.bfloat16)
    kern_lo = (kern_f - kern_hi.astype(jnp.float32)).astype(jnp.bfloat16)
    kern = jnp.concatenate([kern_hi, kern_hi, kern_lo, kern_lo], axis=1)

    total = jnp.zeros((8, BLOCK), jnp.float32)
    for i in range(LOADS):
        spec_loads[i].wait()
        part = spec_v[i * rows : (i + 1) * rows, :].reshape(rows // 8, 8, BLOCK)
        total = total + jnp.sum(part, axis=0)
    etot = jnp.sum(total, axis=0, keepdims=True) * (1.0 / comps)
    diss = jnp.broadcast_to(0.3 * etot, (NFREQ, BLOCK)) * (0.5 + freq * (1.0 / NFREQ))

    def halo(step, c, way):
        first, end = CUTS[step][c], CUTS[step][c + 1]
        into = prv if way == 0 else nxt
        return pltpu.make_async_remote_copy(
            src_ref=own.at[step, pl.ds(first, end - first)],
            dst_ref=into.at[step, pl.ds(first, end - first)],
            send_sem=send_sem.at[step, way, c],
            recv_sem=recv_sem.at[step, way, c],
            device_id={"pts": after if way == 0 else before},
            device_id_type=MESH,
        )

    def send_both(step, c):
        @pl.when(has_after)
        def _():
            halo(step, c, 0).start()

        @pl.when(has_before)
        def _():
            halo(step, c, 1).start()

    def await_both(step, c):
        @pl.when(has_before)
        def _():
            halo(step, c, 0).wait_recv()

        @pl.when(has_after)
        def _():
            halo(step, c, 1).wait_recv()

    def drain(copies):
        @pl.when(has_after)
        def _():
            for step, c in copies:
                halo(step, c, 0).wait_send()

        @pl.when(has_before)
        def _():
            for step, c in copies:
                halo(step, c, 1).wait_send()

    def source(first):
        cells = [spec_v[pl.ds(first + i, NFREQ, stride=NDIR), :] for i in range(PIECE)]
        wide = jnp.concatenate(cells, axis=1)
        wide_hi = wide.astype(jnp.bfloat16)
        wide_lo = (wide - wide_hi.astype(jnp.float32)).astype(jnp.bfloat16)
        mixed = jnp.dot(
            kern,
            jnp.concatenate([wide_hi, wide_lo, wide_hi, wide_lo], axis=0),
            preferred_element_type=jnp.float32,
        )
        for i in range(PIECE):
            d = first + i
            cell = cells[i]
            along = east * trig_s[0, d] + north * trig_s[1, d]
            grow = 0.1 * jnp.maximum(along * half_up - 1.0, 0.0)
            mix = mixed[:, i * BLOCK : (i + 1) * BLOCK]
            own[0, d] = maskf * (cell + cell * (grow - diss) + 0.2 * mix)

    parts = [len(cuts) - 1 for cuts in CUTS]
    for c in range(parts[0]):
        for first in range(CUTS[0][c], CUTS[0][c + 1], PIECE):
            source(first)
        if c == 0:

            @pl.when(grp < EAGER)
            def _():
                meet()

        send_both(0, c)
    @pl.when(grp == 2)
    def _():
        hand(0).start()

    for k in range(1, n_grp):

        @pl.when(grp < k)
        def _():
            pl.semaphore_wait(hello.at[k], 1)
            hand(k).start()

    for load in late_loads:
        load.wait()
    lists = lists_v[...]
    shape = (4, BLOCK)
    slot = lists - (group_points + pos * ghosts)
    column = jnp.zeros(shape, jnp.int32)
    for k in range(ghosts):
        j = blist_s[0, k]
        col = lax.div(j, jnp.int32(coarse_span)) * slots + lax.rem(j, jnp.int32(slots))
        column = jnp.where(slot == k, col, column)
    rel = lists - (pos * BLOCK - BLOCK)
    is_far = lists >= group_points
    place = jnp.where(is_far, 3 * BLOCK + column, rel)

    window = lax.broadcasted_iota(jnp.int32, (4 * BLOCK, BLOCK), 0)
    for r in range(4):
        pick_v[r] = jnp.where(window == place[r : r + 1], 1.0, 0.0).astype(jnp.bfloat16)

    coarse_n[...] = jnp.zeros((comps, BLOCK), jnp.float32)

    def clear(into):
        def clear_one(d, carry):
            for step in range(2):
                into[step, d] = jnp.zeros((NFREQ, BLOCK), jnp.float32)
            return carry

        lax.fori_loop(0, NDIR, clear_one, 0)

    @pl.when(pos == 0)
    def _():
        clear(prv)

    @pl.when(pos == n_pts - 1)
    def _():
        clear(nxt)

    for k in range(n_grp):

        @pl.when(grp != k)
        def _():
            arrival(k).wait_recv()

    stacked = coarse_v[...].reshape(n_grp * slots, comps)
    for t in range(comps // BLOCK):
        tile = stacked[:, t * BLOCK : (t + 1) * BLOCK]
        coarse_n[t * BLOCK : (t + 1) * BLOCK, : n_grp * slots] = jnp.transpose(tile)

    def look_up(step, first, end, places):
        quad = first // QUAD
        lists = [(quad + 1) // 2 % 2, 2 + quad // 2]
        cells = (end - first) * NFREQ
        picks = jnp.concatenate(
            [
                jnp.concatenate(
                    [pick_v[r, p * BLOCK : (p + 1) * BLOCK] for p in places], axis=0
                )
                for r in lists
            ],
            axis=1,
        )
        sources = []
        for p in places:
            if p < 3:
                block = (prv, own, nxt)[p][step, first:end].reshape(cells, BLOCK)
            else:
                block = jnp.concatenate(
                    [coarse_n[pl.ds(d, NFREQ, stride=NDIR), :] for d in range(first, end)],
                    axis=0,
                )
            sources.append(block)
        windows = jnp.concatenate(sources, axis=1)
        high = windows.astype(jnp.bfloat16)
        low = (windows - high.astype(jnp.float32)).astype(jnp.bfloat16)
        both = jnp.dot(
            jnp.concatenate([high, low], axis=0), picks, preferred_element_type=jnp.float32
        )
        return both[:cells] + both[cells:]

    def advect(step, first, end, at_hand=None):
        if at_hand is None:
            found = look_up(step, first, end, (0, 1, 2, 3))
        else:
            found = at_hand + look_up(step, first, end, (0, 2))
        for d in range(first, end):
            cell = own[step, d]
            at = (d - first) * NFREQ
            from_x = found[at : at + NFREQ, :BLOCK]
            from_y = found[at : at + NFREQ, BLOCK:]
            step_x = courant * trig_s[2, d]
            step_y = courant * trig_s[3, d]
            own[step + 1, d] = maskf * (
                cell - step_x * (cell - from_x) - step_y * (cell - from_y)
            )

    got = sent = 0
    edges = sorted({*range(0, NDIR + 1, QUAD), *EARLY})
    for first, end in zip(edges, edges[1:]):
        while got < parts[0] and CUTS[0][got] < end:
            await_both(0, got)
            got += 1
        advect(0, first, end)
        while sent < parts[1] and CUTS[1][sent + 1] <= end:
            send_both(1, sent)
            sent += 1

    rate = jnp.broadcast_to(winds_v[2], (NFREQ, BLOCK)) * turn_factor
    slow = jnp.abs(rate)
    turning_up = rate > 0

    def refract(d):
        mine = own[2, d]
        up = jnp.where(turning_up, own[2, (d - 1) % NDIR], own[2, (d + 1) % NDIR])
        out_ref[pl.ds(d, NFREQ, stride=NDIR), :] = maskf * (mine - slow * (mine - up))

    done = 1
    for c in range(parts[1]):
        at_hand = None
        if c == parts[1] - 1:
            at_hand = look_up(1, CUTS[1][c], CUTS[1][c + 1], (1, 3))
            drain([(0, k) for k in range(parts[0])] + [(1, k) for k in range(c)])
            for k in range(n_grp):

                @pl.when(grp != k)
                def _():
                    hand(k).wait_send()

        await_both(1, c)
        advect(1, CUTS[1][c], CUTS[1][c + 1], at_hand)
        while done < CUTS[1][c + 1] - 1:
            refract(done)
            done += 1
    refract(NDIR - 1)
    refract(0)

    drain([(1, parts[1] - 1)])


def trig_table():
    theta = 2.0 * math.pi * (np.arange(NDIR) + 0.5) / NDIR
    rows = [np.cos(theta), np.sin(theta), np.abs(np.cos(theta)), np.abs(np.sin(theta))]
    return np.stack(rows).astype(np.float32)


def shards(
    n_pts,
    n_grp,
    spectrum,
    coarse_spectra,
    wind_east,
    wind_north,
    refraction,
    freq_kernel,
    sea_mask,
    upwind_lists,
    boundary_list,
):
    comps = spectrum.shape[1]
    slots = coarse_spectra.shape[2]
    ghosts = boundary_list.shape[1]
    anyspace = pl.BlockSpec(memory_space=pl.ANY)
    block = (NDIR, NFREQ, BLOCK)
    out = pl.pallas_call(
        functools.partial(kernel, n_pts, n_grp),
        out_shape=jax.ShapeDtypeStruct((comps, BLOCK), jnp.float32),
        in_specs=[anyspace] * 10,
        out_specs=pl.BlockSpec(memory_space=pltpu.VMEM),
        scratch_shapes=[
            pltpu.VMEM((comps, BLOCK), jnp.float32),
            pltpu.VMEM((3, 1, BLOCK), jnp.float32),
            pltpu.VMEM((NFREQ, NFREQ), jnp.float32),
            pltpu.VMEM((1, BLOCK), jnp.int32),
            pltpu.VMEM((4, BLOCK), jnp.int32),
            pltpu.SMEM((1, ghosts), jnp.int32),
            pltpu.SMEM((4, NDIR), jnp.float32),
            pltpu.VMEM((n_grp, slots, comps), jnp.float32),
            pltpu.VMEM((comps, BLOCK), jnp.float32),
            pltpu.VMEM((4, 4 * BLOCK, BLOCK), jnp.bfloat16),
            pltpu.VMEM((3,) + block, jnp.float32),
            pltpu.VMEM((2,) + block, jnp.float32),
            pltpu.VMEM((2,) + block, jnp.float32),
            pltpu.SemaphoreType.DMA((9,)),
            pltpu.SemaphoreType.DMA((LOADS,)),
            pltpu.SemaphoreType.REGULAR((n_grp,)),
            pltpu.SemaphoreType.DMA((n_grp,)),
            pltpu.SemaphoreType.DMA((n_grp,)),
            pltpu.SemaphoreType.DMA((2, 2, max(map(len, CUTS)) - 1)),
            pltpu.SemaphoreType.DMA((2, 2, max(map(len, CUTS)) - 1)),
        ],
        compiler_params=pltpu.CompilerParams(
            collective_id=0, has_side_effects=True, vmem_limit_bytes=24 * 1024 * 1024
        ),
        name="wave_step",
    )(*[pltpu.with_memory_space_constraint(a, pltpu.HBM) for a in (
        jnp.asarray(trig_table()),
        spectrum[0],
        jnp.transpose(coarse_spectra[0]),
        wind_east,
        wind_north,
        refraction,
        freq_kernel,
        sea_mask,
        upwind_lists[0],
        boundary_list,
    )])
    return out[None]


def solution(mesh):
    placed = (
        P("grp", None, "pts"),
        P("grp", None, "pts"),
        P("grp", "pts"),
        P("grp", "pts"),
        P("grp", "pts"),
        P(),
        P("grp", None),
        P("grp", None, None),
        P("grp", "pts"),
    )
    return jax.shard_map(
        functools.partial(shards, mesh.shape["pts"], mesh.shape["grp"]),
        mesh=mesh,
        in_specs=placed,
        out_specs=P("grp", None, "pts"),
        check_vma=False,
    )
```

```python
import functools
import math

import jax
import jax.numpy as jnp
import numpy as np
from jax import lax
from jax.experimental import pallas as pl
from jax.experimental.pallas import tpu as pltpu
from jax.sharding import PartitionSpec as P

NDIR = 36
NFREQ = 32
BLOCK = 128
QUAD = NDIR // 4
PIECE = 3
CUTS = ((0, 3, 9, 18, 27, 36), (0, 9, 18, 27, 33, 36))
EARLY = ()
LOADS = 2
EAGER = 2
MESH = pl.DeviceIdType.MESH


def kernel(
    n_pts,
    n_grp,
    trig_ref,
    spec_hbm,
    coarse_hbm,
    east_hbm,
    north_hbm,
    turn_hbm,
    kern_hbm,
    mask_hbm,
    lists_hbm,
    blist_hbm,
    out_ref,
    spec_v,
    winds_v,
    kern_v,
    mask_v,
    lists_v,
    blist_s,
    trig_s,
    coarse_v,
    coarse_n,
    pick_v,
    own,
    prv,
    nxt,
    load_sem,
    spec_sem,
    hello,
    co_send,
    co_recv,
    send_sem,
    recv_sem,
):
    pos = lax.axis_index("pts")
    grp = lax.axis_index("grp")
    after = lax.rem(pos + 1, n_pts)
    before = lax.rem(pos + n_pts - 1, n_pts)
    has_before = pos > 0
    has_after = pos < n_pts - 1
    group_points = mask_hbm.shape[1]
    ghosts = blist_hbm.shape[1]
    slots, comps = coarse_hbm.shape
    coarse_span = slots * n_pts

    barrier = pltpu.get_barrier_semaphore()

    @pl.when(has_before)
    def _():
        pl.semaphore_signal(barrier, inc=1, device_id={"pts": before}, device_id_type=MESH)

    @pl.when(has_after)
    def _():
        pl.semaphore_signal(barrier, inc=1, device_id={"pts": after}, device_id_type=MESH)

    for k in range(1, n_grp):

        @pl.when(grp < k)
        def _():
            pl.semaphore_signal(barrier, inc=1, device_id={"grp": k}, device_id_type=MESH)

    here = pl.ds(pl.multiple_of(pos * BLOCK, BLOCK), BLOCK)
    rows = comps // LOADS
    spec_loads = [
        pltpu.make_async_copy(
            spec_hbm.at[pl.ds(i * rows, rows)], spec_v.at[pl.ds(i * rows, rows)], spec_sem.at[i]
        )
        for i in range(LOADS)
    ]
    early_loads = [
        pltpu.make_async_copy(trig_ref, trig_s, load_sem.at[0]),
        pltpu.make_async_copy(east_hbm, winds_v.at[0], load_sem.at[1]),
        pltpu.make_async_copy(north_hbm, winds_v.at[1], load_sem.at[2]),
        pltpu.make_async_copy(kern_hbm, kern_v, load_sem.at[3]),
        pltpu.make_async_copy(mask_hbm.at[:, here], mask_v, load_sem.at[4]),
    ]
    late_loads = [
        pltpu.make_async_copy(coarse_hbm, coarse_v.at[grp], load_sem.at[5]),
        pltpu.make_async_copy(lists_hbm.at[:, here], lists_v, load_sem.at[6]),
        pltpu.make_async_copy(blist_hbm, blist_s, load_sem.at[7]),
        pltpu.make_async_copy(turn_hbm, winds_v.at[2], load_sem.at[8]),
    ]
    for load in spec_loads + early_loads + late_loads:
        load.start()

    def hand(to):
        return pltpu.make_async_remote_copy(
            src_ref=coarse_hbm,
            dst_ref=coarse_v.at[grp],
            send_sem=co_send.at[to],
            recv_sem=co_recv.at[grp],
            device_id={"grp": to},
            device_id_type=MESH,
        )

    def arrival(owner):
        return pltpu.make_async_remote_copy(
            src_ref=coarse_v.at[owner],
            dst_ref=coarse_v.at[owner],
            send_sem=co_send.at[owner],
            recv_sem=co_recv.at[owner],
            device_id={"grp": owner},
            device_id_type=MESH,
        )

    def meet():
        greeted = grp + jnp.where(has_before, 1, 0) + jnp.where(has_after, 1, 0)
        pl.semaphore_wait(barrier, greeted)
        for k in range(n_grp - 1):

            @pl.when(grp > k)
            def _():
                pl.semaphore_signal(
                    hello.at[grp], inc=1, device_id={"grp": k}, device_id_type=MESH
                )

        for k in range(n_grp - 1):

            @pl.when((grp > k) & ((k != 0) | (grp != 2)))
            def _():
                hand(k).start()

    @pl.when(grp >= EAGER)
    def _():
        meet()

    freq = lax.broadcasted_iota(jnp.int32, (NFREQ, BLOCK), 0).astype(jnp.float32)
    half_up = jnp.exp(freq * (0.5 * math.log(1.1)))
    courant = 0.65 * jnp.exp(freq * (-0.5 * math.log(1.1)))
    turn_factor = 0.5 + 0.5 * jnp.exp(freq * (-math.log(1.1)))

    for load in early_loads:
        load.wait()
    maskf = jnp.broadcast_to(mask_v[...].astype(jnp.float32), (NFREQ, BLOCK))
    east = jnp.broadcast_to(winds_v[0], (NFREQ, BLOCK))
    north = jnp.broadcast_to(winds_v[1], (NFREQ, BLOCK))
    kern_f = kern_v[...]
    kern_hi = kern_f.astype(jnp.bfloat16)
    kern_lo = (kern_f - kern_hi.astype(jnp.float32)).astype(jnp.bfloat16)
    kern = jnp.concatenate([kern_hi, kern_hi, kern_lo, kern_lo], axis=1)

    total = jnp.zeros((8, BLOCK), jnp.float32)
    for i in range(LOADS):
        spec_loads[i].wait()
        part = spec_v[i * rows : (i + 1) * rows, :].reshape(rows // 8, 8, BLOCK)
        total = total + jnp.sum(part, axis=0)
    etot = jnp.sum(total, axis=0, keepdims=True) * (1.0 / comps)
    diss = jnp.broadcast_to(0.3 * etot, (NFREQ, BLOCK)) * (0.5 + freq * (1.0 / NFREQ))

    def halo(step, c, way):
        first, end = CUTS[step][c], CUTS[step][c + 1]
        into = prv if way == 0 else nxt
        return pltpu.make_async_remote_copy(
            src_ref=own.at[step, pl.ds(first, end - first)],
            dst_ref=into.at[step, pl.ds(first, end - first)],
            send_sem=send_sem.at[step, way, c],
            recv_sem=recv_sem.at[step, way, c],
            device_id={"pts": after if way == 0 else before},
            device_id_type=MESH,
        )

    def send_both(step, c):
        @pl.when(has_after)
        def _():
            halo(step, c, 0).start()

        @pl.when(has_before)
        def _():
            halo(step, c, 1).start()

    def await_both(step, c):
        @pl.when(has_before)
        def _():
            halo(step, c, 0).wait_recv()

        @pl.when(has_after)
        def _():
            halo(step, c, 1).wait_recv()

    def drain(copies):
        @pl.when(has_after)
        def _():
            for step, c in copies:
                halo(step, c, 0).wait_send()

        @pl.when(has_before)
        def _():
            for step, c in copies:
                halo(step, c, 1).wait_send()

    def source(first):
        cells = [spec_v[pl.ds(first + i, NFREQ, stride=NDIR), :] for i in range(PIECE)]
        wide = jnp.concatenate(cells, axis=1)
        wide_hi = wide.astype(jnp.bfloat16)
        wide_lo = (wide - wide_hi.astype(jnp.float32)).astype(jnp.bfloat16)
        mixed = jnp.dot(
            kern,
            jnp.concatenate([wide_hi, wide_lo, wide_hi, wide_lo], axis=0),
            preferred_element_type=jnp.float32,
        )
        for i in range(PIECE):
            d = first + i
            cell = cells[i]
            along = east * trig_s[0, d] + north * trig_s[1, d]
            grow = 0.1 * jnp.maximum(along * half_up - 1.0, 0.0)
            mix = mixed[:, i * BLOCK : (i + 1) * BLOCK]
            own[0, d] = maskf * (cell + cell * (grow - diss) + 0.2 * mix)

    parts = [len(cuts) - 1 for cuts in CUTS]
    for c in range(parts[0]):
        for first in range(CUTS[0][c], CUTS[0][c + 1], PIECE):
            source(first)
        if c == 0:

            @pl.when(grp < EAGER)
            def _():
                meet()

        send_both(0, c)
    @pl.when(grp == 2)
    def _():
        hand(0).start()

    for k in range(1, n_grp):

        @pl.when(grp < k)
        def _():
            pl.semaphore_wait(hello.at[k], 1)
            hand(k).start()

    for load in late_loads:
        load.wait()
    lists = lists_v[...]
    shape = (4, BLOCK)
    slot = lists - (group_points + pos * ghosts)
    column = jnp.zeros(shape, jnp.int32)
    for k in range(ghosts):
        j = blist_s[0, k]
        col = lax.div(j, jnp.int32(coarse_span)) * slots + lax.rem(j, jnp.int32(slots))
        column = jnp.where(slot == k, col, column)
    rel = lists - (pos * BLOCK - BLOCK)
    is_far = lists >= group_points
    place = jnp.where(is_far, 3 * BLOCK + column, rel)

    window = lax.broadcasted_iota(jnp.int32, (4 * BLOCK, BLOCK), 0)
    for r in range(4):
        pick_v[r] = jnp.where(window == place[r : r + 1], 1.0, 0.0).astype(jnp.bfloat16)

    coarse_n[...] = jnp.zeros((comps, BLOCK), jnp.float32)

    def clear(into):
        def clear_one(d, carry):
            for step in range(2):
                into[step, d] = jnp.zeros((NFREQ, BLOCK), jnp.float32)
            return carry

        lax.fori_loop(0, NDIR, clear_one, 0)

    @pl.when(pos == 0)
    def _():
        clear(prv)

    @pl.when(pos == n_pts - 1)
    def _():
        clear(nxt)

    def look_up(step, first, end, places):
        quad = first // QUAD
        lists = [(quad + 1) // 2 % 2, 2 + quad // 2]
        cells = (end - first) * NFREQ
        picks = jnp.concatenate(
            [
                jnp.concatenate(
                    [pick_v[r, p * BLOCK : (p + 1) * BLOCK] for p in places], axis=0
                )
                for r in lists
            ],
            axis=1,
        )
        sources = []
        for p in places:
            if p < 3:
                block = (prv, own, nxt)[p][step, first:end].reshape(cells, BLOCK)
            else:
                block = jnp.concatenate(
                    [coarse_n[pl.ds(d, NFREQ, stride=NDIR), :] for d in range(first, end)],
                    axis=0,
                )
            sources.append(block)
        windows = jnp.concatenate(sources, axis=1)
        high = windows.astype(jnp.bfloat16)
        low = (windows - high.astype(jnp.float32)).astype(jnp.bfloat16)
        both = jnp.dot(
            jnp.concatenate([high, low], axis=0), picks, preferred_element_type=jnp.float32
        )
        return both[:cells] + both[cells:]

    got = 0
    while got < parts[0] and CUTS[0][got] < QUAD:
        await_both(0, got)
        got += 1
    nearby = look_up(0, 0, QUAD, (0, 1, 2))

    for k in range(n_grp):

        @pl.when(grp != k)
        def _():
            arrival(k).wait_recv()

    stacked = coarse_v[...].reshape(n_grp * slots, comps)
    for t in range(comps // BLOCK):
        tile = stacked[:, t * BLOCK : (t + 1) * BLOCK]
        coarse_n[t * BLOCK : (t + 1) * BLOCK, : n_grp * slots] = jnp.transpose(tile)

    def advect(step, first, end, at_hand=None, left=(0, 2)):
        if at_hand is None:
            found = look_up(step, first, end, (0, 1, 2, 3))
        else:
            found = at_hand + look_up(step, first, end, left)
        for d in range(first, end):
            cell = own[step, d]
            at = (d - first) * NFREQ
            from_x = found[at : at + NFREQ, :BLOCK]
            from_y = found[at : at + NFREQ, BLOCK:]
            step_x = courant * trig_s[2, d]
            step_y = courant * trig_s[3, d]
            own[step + 1, d] = maskf * (
                cell - step_x * (cell - from_x) - step_y * (cell - from_y)
            )

    sent = 0
    edges = sorted({*range(0, NDIR + 1, QUAD), *EARLY})
    for first, end in zip(edges, edges[1:]):
        while got < parts[0] and CUTS[0][got] < end:
            await_both(0, got)
            got += 1
        advect(0, first, end, None if first else nearby, (3,))
        while sent < parts[1] and CUTS[1][sent + 1] <= end:
            send_both(1, sent)
            sent += 1

    rate = jnp.broadcast_to(winds_v[2], (NFREQ, BLOCK)) * turn_factor
    slow = jnp.abs(rate)
    turning_up = rate > 0

    def refract(d):
        mine = own[2, d]
        up = jnp.where(turning_up, own[2, (d - 1) % NDIR], own[2, (d + 1) % NDIR])
        out_ref[pl.ds(d, NFREQ, stride=NDIR), :] = maskf * (mine - slow * (mine - up))

    done = 1
    for c in range(parts[1]):
        at_hand = None
        if c == parts[1] - 1:
            at_hand = look_up(1, CUTS[1][c], CUTS[1][c + 1], (1, 3))
            drain([(0, k) for k in range(parts[0])] + [(1, k) for k in range(c)])
            for k in range(n_grp):

                @pl.when(grp != k)
                def _():
                    hand(k).wait_send()

        await_both(1, c)
        advect(1, CUTS[1][c], CUTS[1][c + 1], at_hand)
        while done < CUTS[1][c + 1] - 1:
            refract(done)
            done += 1
    refract(NDIR - 1)
    refract(0)

    drain([(1, parts[1] - 1)])


def trig_table():
    theta = 2.0 * math.pi * (np.arange(NDIR) + 0.5) / NDIR
    rows = [np.cos(theta), np.sin(theta), np.abs(np.cos(theta)), np.abs(np.sin(theta))]
    return np.stack(rows).astype(np.float32)


def shards(
    n_pts,
    n_grp,
    spectrum,
    coarse_spectra,
    wind_east,
    wind_north,
    refraction,
    freq_kernel,
    sea_mask,
    upwind_lists,
    boundary_list,
):
    comps = spectrum.shape[1]
    slots = coarse_spectra.shape[2]
    ghosts = boundary_list.shape[1]
    anyspace = pl.BlockSpec(memory_space=pl.ANY)
    block = (NDIR, NFREQ, BLOCK)
    out = pl.pallas_call(
        functools.partial(kernel, n_pts, n_grp),
        out_shape=jax.ShapeDtypeStruct((comps, BLOCK), jnp.float32),
        in_specs=[anyspace] * 10,
        out_specs=pl.BlockSpec(memory_space=pltpu.VMEM),
        scratch_shapes=[
            pltpu.VMEM((comps, BLOCK), jnp.float32),
            pltpu.VMEM((3, 1, BLOCK), jnp.float32),
            pltpu.VMEM((NFREQ, NFREQ), jnp.float32),
            pltpu.VMEM((1, BLOCK), jnp.int32),
            pltpu.VMEM((4, BLOCK), jnp.int32),
            pltpu.SMEM((1, ghosts), jnp.int32),
            pltpu.SMEM((4, NDIR), jnp.float32),
            pltpu.VMEM((n_grp, slots, comps), jnp.float32),
            pltpu.VMEM((comps, BLOCK), jnp.float32),
            pltpu.VMEM((4, 4 * BLOCK, BLOCK), jnp.bfloat16),
            pltpu.VMEM((3,) + block, jnp.float32),
            pltpu.VMEM((2,) + block, jnp.float32),
            pltpu.VMEM((2,) + block, jnp.float32),
            pltpu.SemaphoreType.DMA((9,)),
            pltpu.SemaphoreType.DMA((LOADS,)),
            pltpu.SemaphoreType.REGULAR((n_grp,)),
            pltpu.SemaphoreType.DMA((n_grp,)),
            pltpu.SemaphoreType.DMA((n_grp,)),
            pltpu.SemaphoreType.DMA((2, 2, max(map(len, CUTS)) - 1)),
            pltpu.SemaphoreType.DMA((2, 2, max(map(len, CUTS)) - 1)),
        ],
        compiler_params=pltpu.CompilerParams(
            collective_id=0, has_side_effects=True, vmem_limit_bytes=24 * 1024 * 1024
        ),
        name="wave_step",
    )(*[pltpu.with_memory_space_constraint(a, pltpu.HBM) for a in (
        jnp.asarray(trig_table()),
        spectrum[0],
        jnp.transpose(coarse_spectra[0]),
        wind_east,
        wind_north,
        refraction,
        freq_kernel,
        sea_mask,
        upwind_lists[0],
        boundary_list,
    )])
    return out[None]


def solution(mesh):
    placed = (
        P("grp", None, "pts"),
        P("grp", None, "pts"),
        P("grp", "pts"),
        P("grp", "pts"),
        P("grp", "pts"),
        P(),
        P("grp", None),
        P("grp", None, None),
        P("grp", "pts"),
    )
    return jax.shard_map(
        functools.partial(shards, mesh.shape["pts"], mesh.shape["grp"]),
        mesh=mesh,
        in_specs=placed,
        out_specs=P("grp", None, "pts"),
        check_vma=False,
    )
```
